32 devices in a mesh: grp: 2 (over y), seq: 4 (over z), head: 2 (over x), sub: 2 (over core).
Axes of the slice: x: 2, y: 2, z: 4, core: 2. Of those that a mesh axis runs over, the one named last changes fastest.
Arguments:
- hidden: bfloat16 [2048, 4096], P(('grp', 'seq'), ('head', 'sub')), parts along dimension 0, may hold values from -6 to 6
- inner_values: bfloat16 [2048, 8192], P(('grp', 'seq'), ('head', 'sub')), parts along dimension 0, may hold values from -0.29882812 to 0.29882812
- log_decay: float32 [2048, 128], P(('grp', 'seq'), ('head', 'sub')), parts along dimension 0, may hold values from -2 to 0
- skip_gain: float32 [128], P(('head', 'sub')), may hold values from 0.1 to 10
- cotangent: bfloat16 [2048, 8192], P(('grp', 'seq'), ('head', 'sub')), parts along dimension 0, may hold values from -6 to 6
- master: float32 [4096, 2048], P('seq', ('head', 'sub')), may hold values from -0.4 to 0.4
- mask_now: int32 [1024, 2048], P('seq', ('head', 'sub')), may hold values from 0 to 5
- mask_next: int32 [1024, 2048], P('seq', ('head', 'sub')), may hold values from 0 to 5
Outputs:
- ssd_output: bfloat16 [2048, 8192], P(('grp', 'seq'), ('head', 'sub')), parts along dimension 0
- new_weight: float32 [8192, 2048], P(('grp', 'seq'), ('head', 'sub')), parts along dimension 0
- sparse_weight: bfloat16 [8192, 2048], P(('grp', 'seq'), ('head', 'sub')), parts along dimension 0
The draws below stay inside these ranges and needn't reach their ends.
There are 2 independent parts, one for each index of `grp`. The reference program is written for one: setup_inputs(seed, part) draws one part's arguments, and reference() takes and returns one part's arrays. A program takes and returns all parts, laid end to end along the dimension named above; an argument that names none is the same for every part. Nothing has to cross between parts.
All inputs are finite; a program needn't handle non-finite values.
Results may differ from the reference program's by a relative error of at most 0.033.
Values may be sent and summed in bfloat16 or wider, within the bound.
A program may use at most 128 MiB of HBM per device.

```python
import math
from functools import partial
import jax
import jax.numpy as jnp
import numpy as np
from jax import lax

D = 4096
HEADS = 128
HEAD_DIM = 64
STATE = 128
GROUPS = 8
SPAN = 256
TOK_DEV = 256
SEQUENCE_LENGTH = 1024


def draw_log_decay(key, part):
    key_rows = jax.random.split(jax.random.fold_in(key, 11), 10)
    fast_share = 0.5
    fast_heads = jax.random.bernoulli(key_rows[0], fast_share, (HEADS,))
    slow_rate = jnp.exp(jax.random.uniform(key_rows[1], (HEADS,), jnp.float32, math.log(0.02), math.log(0.2))) / SEQUENCE_LENGTH
    fast_rate = jax.random.uniform(key_rows[2], (HEADS,), jnp.float32, 2.3 / 50.0, 2.3 / 30.0)
    head_decay_rate = jnp.where(fast_heads, fast_rate, slow_rate)
    block_multiplier = jnp.exp(jax.random.uniform(key_rows[3], (SEQUENCE_LENGTH // TOK_DEV, 1), jnp.float32, -math.log(2.0), math.log(2.0)))
    block_multiplier = jnp.repeat(block_multiplier, TOK_DEV, axis=0)
    jitter_amplitude = jnp.exp(jax.random.uniform(key_rows[4], (SEQUENCE_LENGTH, HEADS), jnp.float32, math.log(0.5), math.log(1.5)))
    window_length = min(4 * TOK_DEV, SEQUENCE_LENGTH)
    windows = SEQUENCE_LENGTH // window_length
    window_blocks = window_length // SPAN
    block_pick = jax.random.randint(key_rows[5], (windows,), 0, window_blocks)
    offset_pick = jax.random.randint(key_rows[6], (windows,), 0, SPAN - 1)
    window_index = jnp.arange(windows, dtype=jnp.int32)
    first_position = window_index * window_length + block_pick * SPAN + offset_pick
    paired = window_index % 2 == 0
    paired_first = jax.random.uniform(key_rows[7], (windows,), jnp.float32, 1.155, 1.25)
    single_height = jax.random.uniform(key_rows[8], (windows,), jnp.float32, 1.3, 1.7)
    paired_second = jax.random.uniform(key_rows[9], (windows,), jnp.float32, 1.155, 1.25)
    first_height = jnp.where(paired, paired_first, single_height)
    second_height = jnp.where(paired, paired_second, 0.0)
    target_positions = jnp.arange(SEQUENCE_LENGTH, dtype=jnp.int32)
    first_hits = jnp.where(target_positions[:, None] == first_position[None, :], first_height[None, :], 0.0)
    second_hits = jnp.where(target_positions[:, None] == first_position[None, :] + 1, second_height[None, :], 0.0)
    spike_events = jnp.sum(first_hits + second_hits, axis=1)
    return -(head_decay_rate[None, :] * block_multiplier * jitter_amplitude) - spike_events[:, None]


def plant(values, rng, low, largest):
    shape = values.shape
    place = [jax.random.randint(jax.random.fold_in(rng, axis), (), 0, shape[axis]) for axis in range(len(shape))]
    values = values.at[tuple(place)].set(low)
    longest = shape.index(max(shape))
    place[longest] = (place[longest] + 1) % shape[longest]
    return values.at[tuple(place)].set(largest)


def raised(values, stream_key, source, target, blocks, factor):
    owner, partner = [(jnp.arange(values.shape[axis_at]) // (values.shape[axis_at] // blocks)).reshape([-1 if axis == axis_at else 1 for axis in range(values.ndim)]) for axis_at in (source, target)]
    chosen = jax.random.permutation(stream_key, blocks)[partner]
    strong = (owner == chosen) | (owner == (partner + blocks // 2) % blocks)
    return jnp.where(strong, factor * values, values)


def steps_of(stream_key, dims, cuts, least, top_value):
    level = 1.0
    for axis_at, parts in cuts:
        steps = jax.random.uniform(jax.random.fold_in(jax.random.fold_in(stream_key, 6), axis_at), (parts,), jnp.float32, least / len(cuts), top_value / len(cuts))
        level = level * jnp.repeat(jnp.exp(steps), dims[axis_at] // parts).reshape((-1,) + (1,) * (len(dims) - 1 - axis_at))
    return level


def noise(stream_key, shape, scale, most, cuts=(), held_as=jnp.bfloat16):
    level = steps_of(stream_key, shape, cuts, -0.22, 0.18) if cuts else 1.0
    values = jax.random.normal(stream_key, shape, jnp.float32) * scale * level
    return jnp.minimum(jnp.maximum(values, -most), most).astype(held_as)


def bell_draw_with(key, dims, scale, reach, cuts, heavy, kind=jnp.bfloat16):
    result = scale * jax.random.normal(key, dims, jnp.float32)
    if cuts:
        result = result * steps_of(key, dims, cuts, -0.22, 0.18)
    return jnp.clip(raised(result, jax.random.fold_in(key, 3), *heavy), -reach, reach).astype(kind)


def setup_inputs(seed: int = 0, part: int = 0) -> dict:
    keys = jax.random.split(jax.random.key(seed), 9)
    part_keys = jax.random.split(jax.random.fold_in(keys[8], part), 9)
    hidden = bell_draw_with(part_keys[0], (SEQUENCE_LENGTH, D), 1.0, 6.0, ((0, 4), (1, 4)), (0, 1, 4, 2.0))
    inner_values = noise(part_keys[1], (SEQUENCE_LENGTH, HEADS * HEAD_DIM), 0.05, 0.29882812, ((0, 4), (1, 4)))
    log_decay = draw_log_decay(jax.random.fold_in(jax.random.fold_in(keys[8], part), 71), part)
    skip_gain = jnp.clip(jnp.exp(math.log(10.0) - 4.6051702 * jax.random.uniform(keys[3], (HEADS,), jnp.float32) ** steps_of(keys[3], (HEADS,), ((0, 4),), -0.2, 0.2)), 0.1, 10.0)
    cotangent = noise(part_keys[4], (SEQUENCE_LENGTH, HEADS * HEAD_DIM), 1.0, 6.0, ((0, 4), (1, 4)))
    master = noise(keys[5], (D, 2 * GROUPS * STATE), 0.1, 0.4, ((0, 4), (1, 4)), jnp.float32)
    mask_now = plant(jax.random.randint(keys[6], (D // 4, 2 * GROUPS * STATE), 0, 6), jax.random.fold_in(keys[6], 1), 0, 5).astype(jnp.int32)
    mask_next = plant(jax.random.randint(keys[7], (D // 4, 2 * GROUPS * STATE), 0, 6), jax.random.fold_in(keys[7], 1), 0, 5).astype(jnp.int32)
    return dict(hidden=hidden, inner_values=inner_values, log_decay=log_decay, skip_gain=skip_gain, cotangent=cotangent, master=master, mask_now=mask_now, mask_next=mask_next)


PAIR_TABLE = np.array([[1, 1, 0, 0], [1, 0, 1, 0], [1, 0, 0, 1], [0, 1, 1, 0], [0, 1, 0, 1], [0, 0, 1, 1]], np.float32)
LEARN_RATE = 0.05
WEIGHT_DECAY = 10.0

def expand_mask(pattern_ids):
    group_rows, columns = pattern_ids.shape
    patterns = jnp.arange(6, dtype=jnp.int32)
    chosen = (pattern_ids[:, None, :] == patterns[None, :, None]).astype(jnp.float32)
    kept_mask = jnp.einsum('rpc,pk->rkc', chosen, jnp.asarray(PAIR_TABLE, jnp.float32))
    return kept_mask.reshape(group_rows * 4, columns)

def round_low(values):
    return lax.optimization_barrier(values.astype(jnp.bfloat16)).astype(jnp.float32)

def block_terms(log_block):
    cumulative = jnp.cumsum(log_block, axis=0)
    block_end = cumulative[-1]
    target_positions = jnp.arange(log_block.shape[0])
    causal = target_positions[:, None] >= target_positions[None, :]
    per_head = jnp.moveaxis(cumulative, 0, -1)
    spread = per_head[..., :, None] - per_head[..., None, :]
    decays = jnp.where(causal, jnp.exp(jnp.where(causal, spread, 0.0)), 0.0)
    return (cumulative, block_end, decays)

def forward_block(skip_group, running_state, inputs):
    value_block, log_block, write_block, read_block = inputs
    cumulative, block_end, decays = block_terms(log_block)
    scores = jnp.dot(read_block, write_block.T, preferred_element_type=jnp.float32)
    mixing = round_low(scores[None] * decays)
    value_wide = value_block.astype(jnp.float32)
    local_mix = jnp.einsum('hts,shp->thp', mixing, value_wide)
    write_low = round_low(write_block.astype(jnp.float32)[:, None, :] * jnp.exp(block_end[None, :] - cumulative)[:, :, None])
    read_low = round_low(read_block.astype(jnp.float32)[:, None, :] * jnp.exp(cumulative)[:, :, None])
    start_low = round_low(running_state)
    carried_in = jnp.einsum('thn,hnp->thp', read_low, start_low)
    output = (local_mix + carried_in + skip_group[None, :, None] * value_wide).astype(jnp.bfloat16)
    block_state = jnp.einsum('shn,shp->hnp', write_low, value_wide)
    new_state = jnp.exp(block_end)[:, None, None] * running_state + block_state
    return (new_state, (output, start_low.astype(jnp.bfloat16)))

def backward_block(adjoint, inputs):
    value_block, log_block, write_block, read_block, cotan_block, start_low = inputs
    cumulative, block_end, decays = block_terms(log_block)
    value_wide = value_block.astype(jnp.float32)
    cotan_wide = cotan_block.astype(jnp.float32)
    write_wide = write_block.astype(jnp.float32)
    read_wide = read_block.astype(jnp.float32)
    products = jnp.einsum('thp,shp->hts', cotan_wide, value_wide)
    back_mix = round_low(products * decays)
    grad_read = jnp.einsum('hts,sn->tn', back_mix, write_wide)
    grad_write = jnp.einsum('hts,tn->sn', back_mix, read_wide)
    adjoint_low = round_low(adjoint)
    grad_write = grad_write + lax.optimization_barrier(jnp.sum(jnp.einsum('shp,hnp->shn', value_wide, adjoint_low) * jnp.exp(block_end[None, :] - cumulative)[:, :, None], axis=1))
    grad_read = grad_read + lax.optimization_barrier(jnp.sum(jnp.einsum('thp,hnp->thn', cotan_wide, start_low.astype(jnp.float32)) * jnp.exp(cumulative)[:, :, None], axis=1))
    read_low = round_low(read_wide[:, None, :] * jnp.exp(cumulative)[:, :, None])
    new_adjoint = jnp.einsum('thn,thp->hnp', read_low, cotan_wide) + jnp.exp(block_end)[:, None, None] * adjoint
    return (new_adjoint, jnp.concatenate([grad_write, grad_read], axis=1).astype(jnp.bfloat16))

def group_pass(inputs):
    value_group, logs_group, cotan_group, proj_group, skip_group = inputs
    blocks = SEQUENCE_LENGTH // SPAN
    heads_group = HEADS // GROUPS
    value_blocks = value_group.reshape(blocks, SPAN, heads_group, HEAD_DIM)
    cotan_blocks = cotan_group.reshape(blocks, SPAN, heads_group, HEAD_DIM)
    log_blocks = logs_group.reshape(blocks, SPAN, heads_group)
    write_blocks = proj_group[:, :STATE].reshape(blocks, SPAN, STATE)
    read_blocks = proj_group[:, STATE:].reshape(blocks, SPAN, STATE)
    zero_state = jnp.zeros((heads_group, STATE, HEAD_DIM), jnp.float32)
    _, (outputs, starts) = lax.scan(partial(forward_block, skip_group), zero_state, (value_blocks, log_blocks, write_blocks, read_blocks))
    _, grads = lax.scan(backward_block, zero_state, (value_blocks, log_blocks, write_blocks, read_blocks, cotan_blocks, starts), reverse=True)
    return (outputs.reshape(SEQUENCE_LENGTH, heads_group, HEAD_DIM), grads.reshape(SEQUENCE_LENGTH, 2 * STATE))

def reference(hidden, inner_values, log_decay, skip_gain, cotangent, master, mask_now, mask_next):
    weight_scale = 2.0 / math.sqrt(D)
    keep_now = expand_mask(mask_now)
    effective = (master * keep_now * weight_scale).astype(jnp.bfloat16)
    projected = jnp.dot(hidden, effective, preferred_element_type=jnp.float32).astype(jnp.bfloat16)
    heads_group = HEADS // GROUPS
    value_groups = jnp.moveaxis(inner_values.reshape(SEQUENCE_LENGTH, GROUPS, heads_group, HEAD_DIM), 1, 0)
    cotan_groups = jnp.moveaxis(cotangent.reshape(SEQUENCE_LENGTH, GROUPS, heads_group, HEAD_DIM), 1, 0)
    log_groups = jnp.moveaxis(log_decay.reshape(SEQUENCE_LENGTH, GROUPS, heads_group), 1, 0)
    proj_groups = jnp.moveaxis(projected.reshape(SEQUENCE_LENGTH, GROUPS, 2 * STATE), 1, 0)
    skip_groups = skip_gain.reshape(GROUPS, heads_group)
    outputs, grads = lax.map(group_pass, (value_groups, log_groups, cotan_groups, proj_groups, skip_groups))
    ssd_output = jnp.moveaxis(outputs, 0, 1).reshape(SEQUENCE_LENGTH, HEADS * HEAD_DIM)
    grad_proj = jnp.moveaxis(grads, 0, 1).reshape(SEQUENCE_LENGTH, GROUPS * 2 * STATE)
    hidden_blocks = hidden.reshape(SEQUENCE_LENGTH // TOK_DEV, TOK_DEV, D)
    grad_blocks = grad_proj.reshape(SEQUENCE_LENGTH // TOK_DEV, TOK_DEV, GROUPS * 2 * STATE)

    def add_block(running, inputs):
        rows_in, grads_in = inputs
        term = jnp.dot(rows_in.T, grads_in, preferred_element_type=jnp.float32) * weight_scale
        return (running + round_low(term), None)
    gradient, _ = lax.scan(add_block, jnp.zeros(master.shape, jnp.float32), (hidden_blocks, grad_blocks))
    new_weight = master - LEARN_RATE * (gradient + WEIGHT_DECAY * (1.0 - keep_now) * master)
    sparse_weight = (new_weight * expand_mask(mask_next)).astype(jnp.bfloat16)
    return (ssd_output, new_weight, sparse_weight)
```

```python
import functools
import math

import jax
import jax.numpy as jnp
from jax import lax
from jax.experimental import pallas as pl
from jax.experimental.pallas import tpu as pltpu
from jax.sharding import PartitionSpec as P

STATE = 128
LEARN_RATE = 0.05
WEIGHT_DECAY = 10.0
LANES = 128
MESH = pl.DeviceIdType.MESH
F32 = jnp.float32
BF16 = jnp.bfloat16

ROWS_FIRST = (((0,), (0,)), ((), ()))
LANES_BOTH = (((1,), (1,)), ((), ()))


def dot(a, b, dims=None):
    if dims is None:
        dims = (((1,), (0,)), ((), ()))
    return lax.dot_general(a, b, dims, preferred_element_type=F32)


def pattern_code(ids):
    code = jnp.where(ids == 0, 3.0, 12.0)
    code = jnp.where(ids == 1, 5.0, code)
    code = jnp.where(ids == 2, 9.0, code)
    code = jnp.where(ids == 3, 6.0, code)
    return jnp.where(ids == 4, 10.0, code)


def kernel(
    n, heads_axis, subs, scale,
    hid, x_in, dy_in, log_ref, skip_ref, master_in, now_in, next_in,
    out_hbm, new_hbm, sparse_hbm,
    out, new_ref, sparse_ref,
    xv, dyv, master, now, nxt, code, eff,
    held, held_t, part_out, part_in, acc,
    cum, cum_t, decay, mix_sum, xs, ys, ec, write, read, scores,
    s_loc, a_loc, s_out, a_out, s_in, a_in, g_write, g_read, g_all, grad, local,
    relay, load_sem, own_sem, send_r, recv_r, send1, recv1, send2, recv2, send3, recv3, send_p, recv_p,
    send_s, recv_s, send_a, recv_a, send_g, recv_g, store_sem,
):
    hs = heads_axis * subs
    tokens = hid.shape[0]
    part = tokens // hs
    rows, columns = master.shape
    per_device = hid.shape[1] // rows
    groups = columns // (2 * STATE)
    width = xv.shape[1]
    heads = log_ref.shape[0]
    head_width = width // heads
    in_pair = LANES // head_width
    pairs = width // LANES
    chunks, _, chunk_width = xs.shape
    chunk_pairs = chunk_width // LANES
    group_chunks = chunks // groups
    group_pairs = pairs // groups

    z = lax.axis_index("seq")
    sub = lax.axis_index("sub")
    h = lax.axis_index("head") * subs + sub
    me = z * hs + h
    upper_half = 2 * z // n
    inward = upper_half * (n - 1 - z) + (1 - upper_half) * z

    def at_least(a, b):
        return (a + 2 * n - b) // (2 * n)

    def farthest(i):
        both = 1 - at_least(i, 2 * inward)
        step = both * (i // 2) + (1 - both) * (i - inward)
        down = both * (i % 2)
        to = down * step + (1 - down) * (n - 1 - step)
        return upper_half * (n - 1 - to) + (1 - upper_half) * to

    def nearest(i):
        return farthest(n - 1 - i)

    def place(zz, hh):
        return {"seq": zz, "head": hh // subs, "sub": hh % subs}

    loads = [
        pltpu.make_async_copy(src, dst, load_sem.at[i])
        for i, (src, dst) in enumerate(
            ((x_in, xv), (dy_in, dyv), (now_in, now), (next_in, nxt), (master_in, master))
        )
    ]
    for load in loads:
        load.start()

    barrier = pltpu.get_barrier_semaphore()

    def same_line(i):
        return place(i // subs, h - sub + i % subs)

    def greet_line(i, carry):
        @pl.when(i != z * subs + sub)
        def _():
            pl.semaphore_signal(barrier, inc=1, device_id=same_line(i), device_id_type=MESH)
        return carry

    def across(k):
        return place(z, (h // subs + k) % heads_axis * subs + sub)

    for k in range(1, heads_axis):
        pl.semaphore_signal(barrier, inc=1, device_id=across(k), device_id_type=MESH)
    lax.fori_loop(0, n * subs, greet_line, 0)
    pl.semaphore_wait(barrier, n * subs - 1 + heads_axis - 1)

    def quarter(t):
        return pl.ds(pl.multiple_of(t * part, part), part)

    def plane(j):
        return pl.ds(pl.multiple_of(j * rows, rows), rows)

    def relay_copy(k, j, c):
        at = ((k - 1) * per_device + j) * subs + c
        t = (h // subs + k) % heads_axis * subs + c
        return pltpu.make_async_remote_copy(
            hid.at[quarter(t), plane(j)], relay.at[at], send_r.at[at], recv_r.at[at],
            device_id=across(k), device_id_type=MESH,
        )

    def feature_parts(k, j, c):
        t = h - sub + c
        source = ((h // subs + heads_axis - k) % heads_axis) * subs + sub
        zt = source * per_device + j
        if k == 0:
            src = hid.at[quarter(t), plane(j)]
        else:
            src = relay.at[((k - 1) * per_device + j) * subs + c]
        dst = held.at[z, quarter(t), :]
        mine = jnp.logical_and(zt == z, c == sub)
        local_copy = pltpu.make_async_copy(src, dst, own_sem.at[0])
        remote = pltpu.make_async_remote_copy(
            src, dst, send1.at[(k * per_device + j) * subs + c], recv1.at[z],
            device_id=place(zt, t), device_id_type=MESH,
        )
        return mine, local_copy, remote

    def send_features(k, j, c):
        mine, local_copy, remote = feature_parts(k, j, c)

        @pl.when(mine)
        def _():
            local_copy.start()

        @pl.when(jnp.logical_not(mine))
        def _():
            remote.start()

    def forward_features(c):
        def forward(j, carry):
            for k in range(1, heads_axis):
                relay_copy(k, j, c).wait_recv()
                send_features(k, j, c)
            return carry

        lax.fori_loop(0, per_device, forward, 0)

    def first_sends(i, carry):
        c, j = i // per_device, i % per_device
        for k in range(1, heads_axis):
            relay_copy(k, j, c).start()
        send_features(0, j, c)
        return carry

    lax.fori_loop(0, per_device * subs, first_sends, 0)

    at_row = lax.broadcasted_iota(jnp.int32, (tokens, tokens), 0)
    at_lane = lax.broadcasted_iota(jnp.int32, (tokens, tokens), 1)
    upper = (at_row <= at_lane).astype(F32)
    cum_t[...] = jnp.zeros_like(cum_t)
    cum_t[:heads, :] = lax.dot_general(
        log_ref[...], upper, (((1,), (0,)), ((), ())),
        precision=lax.Precision.HIGHEST, preferred_element_type=F32,
    )
    cum[...] = cum_t[...].T

    forward_features(0)
    loads[2].wait()
    loads[3].wait()
    loads[4].wait()
    small = (pattern_code(now[...]) + 16.0 * pattern_code(nxt[...])).astype(BF16)
    tile = min(rows, 128)

    def effective(i, carry):
        at = pl.ds(pl.multiple_of(i * tile, tile), tile)
        row = i * tile + lax.broadcasted_iota(jnp.int32, (tile, rows // 4), 0)
        spot = lax.broadcasted_iota(jnp.int32, (tile, rows // 4), 1)
        spread = (row // 4 == spot).astype(BF16)
        both = dot(spread, small)
        code[at, :] = both.astype(BF16)
        place_in = lax.broadcasted_iota(jnp.int32, (tile, columns), 0) % 4
        keep = ((both.astype(jnp.int32) >> place_in) & 1).astype(F32)
        eff[at, :] = (master[at, :] * keep * scale).astype(BF16)
        return carry

    lax.fori_loop(0, rows // tile, effective, 0)

    for c in range(1, subs):
        forward_features(c)
    loads[0].wait()
    loads[1].wait()
    mix_sum[...] = jnp.zeros_like(mix_sum)
    lane = lax.broadcasted_iota(jnp.int32, (tokens, LANES), 1)
    head_masks = [
        (lane // head_width == j).astype(BF16) for j in range(in_pair)
    ]

    def head_column(hh):
        return jnp.sum(jnp.where(lane == hh, cum[...], 0.0), axis=1, keepdims=True)

    def independent(p, carry):
        at = pl.ds(pl.multiple_of(p * LANES, LANES), LANES)
        c = p // chunk_pairs
        inner = pl.ds(pl.multiple_of((p % chunk_pairs) * LANES, LANES), LANES)
        x2, d2 = xv[:, at], dyv[:, at]
        total = jnp.zeros((tokens, tokens), F32)
        across = jnp.zeros((tokens, LANES), F32)
        for j in range(in_pair):
            hh = p * in_pair + j
            column = head_column(hh)
            across = jnp.where(lane // head_width == j, column, across)
            spread = column - cum_t[pl.ds(hh, 1), :]
            factor = jnp.exp(jnp.where(at_row >= at_lane, spread, -1e30))
            decay[hh] = factor
            total = total + dot(d2 * head_masks[j], x2, LANES_BOTH) * factor
        g = p // group_pairs
        mix_sum[g] = mix_sum[g] + total
        grown = jnp.exp(across)
        left = jnp.exp(across[tokens - 1 :, :] - across)
        ec[c, :, inner] = grown
        xs[c, :, inner] = (x2.astype(F32) * left).astype(BF16)
        ys[c, :, inner] = (d2.astype(F32) * grown).astype(BF16)
        return carry

    lax.fori_loop(0, pairs, independent, 0)

    from_h = z // per_device

    def share(zp, k):
        head = (h // subs + k) % heads_axis
        return pltpu.make_async_remote_copy(
            held.at[zp, quarter(h), :], held.at[zp, quarter(h), :],
            send2.at[zp * heads_axis + k], recv2.at[zp * heads_axis + k],
            device_id=place(z, head * subs + sub), device_id_type=MESH,
        )

    def shared(zp, k):
        t = ((h // subs + heads_axis - k) % heads_axis) * subs + sub
        return pltpu.make_async_remote_copy(
            held.at[zp, quarter(t), :], held.at[zp, quarter(t), :],
            send2.at[zp * heads_axis + k], recv2.at[zp * heads_axis + k],
            device_id=place(z, t), device_id_type=MESH,
        )

    def hand_over(zp, k, from_sub, to_sub):
        t = ((h // subs + heads_axis - k) % heads_axis) * subs + from_sub
        return pltpu.make_async_remote_copy(
            held.at[zp, quarter(t), :], held.at[zp, quarter(t), :],
            send3.at[zp * heads_axis + k], recv3.at[zp * heads_axis + k],
            device_id=place(z, h - sub + to_sub), device_id_type=MESH,
        )

    def up_copy(t, g):
        return pltpu.make_async_remote_copy(
            part_out.at[g, t], part_in.at[g, t],
            send_p.at[g * n + t], recv_p.at[g * (n + 1) + t],
            device_id=place(z + 1, h), device_id_type=MESH,
        )

    def down_copy(t, g):
        last = at_least(t, z - 1)
        slot = t + last * (n - t)
        return pltpu.make_async_remote_copy(
            part_out.at[g, t], part_in.at[g, slot],
            send_p.at[g * n + t], recv_p.at[g * (n + 1) + slot],
            device_id=place(z - 1, h), device_id_type=MESH,
        )

    def part_arrival(slot, g):
        pltpu.make_async_remote_copy(
            part_in.at[g, slot], part_in.at[g, slot],
            send_p.at[0], recv_p.at[g * (n + 1) + slot],
            device_id=across(1), device_id_type=MESH,
        ).wait_recv()

    def own_product(g):
        acc[g] = dot(held[z], eff[:, g * 2 * STATE : (g + 1) * 2 * STATE])

    def product(t, g):
        result = dot(held[t], eff[:, g * 2 * STATE : (g + 1) * 2 * STATE])
        first = jnp.logical_or(
            jnp.logical_and(z == 0, t > z), jnp.logical_and(z == n - 1, t < z)
        )

        @pl.when(first)
        def _():
            part_out[g, t] = result.astype(BF16)

        @pl.when(jnp.logical_not(first))
        def _():
            part_arrival(t, g)
            part_out[g, t] = (result + part_in[g, t].astype(F32)).astype(BF16)

        @pl.when(t > z)
        def _():
            up_copy(t, g).start()

        @pl.when(t < z)
        def _():
            down_copy(t, g).start()

    def token_block(i):
        return ((i + n - 1) // n) * farthest((i + n - 1) % n) + (1 - (i + n - 1) // n) * z

    def project(d, carry):
        @pl.when(d < n)
        def _():
            zp = token_block(d)
            mine = jnp.logical_and(zp == z, from_h % subs == sub)

            @pl.when(mine)
            def _():
                pltpu.make_async_copy(
                    held.at[zp, quarter(h), :], held.at[zp, quarter(h), :], own_sem.at[0]
                ).wait()

            @pl.when(jnp.logical_not(mine))
            def _():
                pltpu.make_async_remote_copy(
                    held.at[zp, quarter(h), :], held.at[zp, quarter(h), :],
                    send1.at[0], recv1.at[zp],
                    device_id=place(z, h - sub + 1 - sub), device_id_type=MESH,
                ).wait_recv()

            for k in range(1, heads_axis):
                share(zp, k).start()
            hand_over(zp, 0, sub, 1 - sub).start()

        @pl.when(jnp.logical_and(d >= 1, d < n + 1))
        def _():
            zp = token_block(d - 1)
            for k in range(1, heads_axis):
                shared(zp, k).wait_recv()
                hand_over(zp, k, sub, 1 - sub).start()

        @pl.when(d >= 2)
        def _():
            zp = token_block(d - 2)
            for k in range(heads_axis):
                hand_over(zp, k, 1 - sub, sub).wait_recv()

            @pl.when(d == 2)
            def _():
                own_product(0)

            @pl.when(d > 2)
            def _():
                product(zp, 0)
        return carry

    lax.fori_loop(0, n + 2, project, 0)
    for g in range(1, groups):
        own_product(g)

        def later_product(i, carry):
            product(farthest(i), g)
            return carry

        lax.fori_loop(0, n - 1, later_product, 0)

    def turn(zp, carry):
        held_t[zp] = held[zp].T
        return carry

    lax.fori_loop(0, n, turn, 0)

    def state_copy(c):
        return pltpu.make_async_remote_copy(
            s_out.at[c], s_in.at[c], send_s.at[c], recv_s.at[c],
            device_id=place(lax.rem(z + 1, n), h), device_id_type=MESH,
        )

    def adjoint_copy(c):
        return pltpu.make_async_remote_copy(
            a_out.at[c], a_in.at[c], send_a.at[c], recv_a.at[c],
            device_id=place(lax.rem(z + n - 1, n), h), device_id_type=MESH,
        )

    def block_states(c, carry):
        g = c // group_chunks
        state = dot(write[g], xs[c], ROWS_FIRST)
        adjoint = dot(read[g], ys[c], ROWS_FIRST)
        s_loc[c] = state
        a_loc[c] = adjoint

        @pl.when(z == 0)
        def _():
            s_in[c] = jnp.zeros_like(s_in[c])
            s_out[c] = state.astype(BF16)
            state_copy(c).start()

        @pl.when(z == n - 1)
        def _():
            a_in[c] = jnp.zeros_like(a_in[c])
            a_out[c] = adjoint.astype(BF16)
            adjoint_copy(c).start()
        return carry

    def mixing(p, carry):
        at = pl.ds(pl.multiple_of(p * LANES, LANES), LANES)
        x2 = xv[:, at]
        g = p // group_pairs
        gain = jnp.zeros((tokens, LANES), F32)
        result = jnp.zeros((tokens, LANES), F32)
        for j in range(in_pair):
            hh = p * in_pair + j
            gain = jnp.where(lane // head_width == j, skip_ref[hh], gain)
            mix = (scores[g] * decay[hh]).astype(BF16)
            result = result + dot(mix, x2 * head_masks[j])
        local[:, at] = result + gain * x2.astype(F32)
        return carry

    def pass_state(c):
        @pl.when(z > 0)
        def _():
            state_copy(c).wait_recv()

            @pl.when(z < n - 1)
            def _():
                end = ec[c, tokens - 1 :, :]
                s_out[c] = (end * s_in[c].astype(F32) + s_loc[c]).astype(BF16)
                state_copy(c).start()

    def pass_adjoint(c):
        @pl.when(z < n - 1)
        def _():
            adjoint_copy(c).wait_recv()

            @pl.when(z > 0)
            def _():
                end = ec[c, tokens - 1 :, :]
                a_out[c] = (end * a_in[c].astype(F32) + a_loc[c]).astype(BF16)
                adjoint_copy(c).start()

    def gradient_copy(zp, g, up):
        to = z + 1 if up else z - 1
        at = zp * groups + g
        return pltpu.make_async_remote_copy(
            g_all.at[zp, g], g_all.at[zp, g],
            send_g.at[up * n * groups + at], recv_g.at[at],
            device_id=place(to, h), device_id_type=MESH,
        )

    def pass_gradient(zp, g):
        @pl.when(jnp.logical_and(zp <= z, z < n - 1))
        def _():
            gradient_copy(zp, g, 1).start()

        @pl.when(jnp.logical_and(zp >= z, z > 0))
        def _():
            gradient_copy(zp, g, 0).start()

    def take_gradient(zp, g):
        at = zp * groups + g
        pltpu.make_async_remote_copy(
            g_all.at[zp, g], g_all.at[zp, g], send_g.at[0], recv_g.at[at],
            device_id=across(1), device_id_type=MESH,
        ).wait_recv()
        pass_gradient(zp, g)

    def pass_first(c):
        @pl.when(2 * z < n)
        def _():
            pass_state(c)

        @pl.when(2 * z >= n)
        def _():
            pass_adjoint(c)

    def chain_end(c, g):
        @pl.when(2 * z < n)
        def _():
            pass_adjoint(c)

        @pl.when(2 * z >= n)
        def _():
            pass_state(c)

        g_read[g] = g_read[g] + dot(ys[c], s_in[c], LANES_BOTH)
        g_write[g] = g_write[g] + dot(xs[c], a_in[c], LANES_BOTH)

    def send_gradient(g):
        g_all[z, g, :, :STATE] = g_write[g].astype(BF16)
        g_all[z, g, :, STATE:] = g_read[g].astype(BF16)
        pass_gradient(z, g)

    def begin(g):
        @pl.when(z > 0)
        def _():
            part_arrival(z, g)
            acc[g] = acc[g] + part_in[g, z].astype(F32)

        @pl.when(z < n - 1)
        def _():
            part_arrival(n, g)
            acc[g] = acc[g] + part_in[g, n].astype(F32)

        write[g] = acc[g, :, :STATE].astype(BF16)
        read[g] = acc[g, :, STATE:].astype(BF16)
        lax.fori_loop(g * group_chunks, (g + 1) * group_chunks, block_states, 0)
        scores[g] = dot(read[g], write[g], LANES_BOTH)
        mixed = mix_sum[g].astype(BF16)
        g_write[g] = dot(mixed, read[g], ROWS_FIRST)
        g_read[g] = dot(mixed, write[g])

    begin(0)
    early = min(group_chunks, n)
    for g in range(groups + 1):

        def chain(i, carry):
            if g > 0:
                chain_end((g - 1) * group_chunks + i, g - 1)
            if g < groups:
                c = g * group_chunks + i
                pass_first(c)
                lax.fori_loop(c * chunk_pairs, (c + 1) * chunk_pairs, mixing, 0)
            elif g > 1:

                @pl.when(jnp.logical_and(i > 0, i < early))
                def _():
                    take_gradient(nearest(i), g - 2)
            return carry

        lax.fori_loop(0, group_chunks, chain, 0)
        if g > 0:
            send_gradient(g - 1)
        if g + 1 < groups:
            begin(g + 1)

    def finish(c, carry):
        at = pl.ds(pl.multiple_of(c * chunk_width, chunk_width), chunk_width)
        carried = dot(read[c // group_chunks], s_in[c])
        out[:, at] = (local[:, at] + ec[c] * carried).astype(BF16)
        return carry

    def weight_stores(g):
        cols = pl.ds(g * 2 * STATE, 2 * STATE)
        return (
            pltpu.make_async_copy(
                new_ref.at[:, cols], new_hbm.at[:, cols], store_sem.at[1 + 2 * g]
            ),
            pltpu.make_async_copy(
                sparse_ref.at[:, cols], sparse_hbm.at[:, cols], store_sem.at[2 + 2 * g]
            ),
        )

    def update(g):
        cols = slice(g * 2 * STATE, (g + 1) * 2 * STATE)

        def rows_of(i, carry):
            at = pl.ds(pl.multiple_of(i * tile, tile), tile)
            place_in = lax.broadcasted_iota(jnp.int32, (tile, 2 * STATE), 0) % 4
            bits = code[at, cols].astype(F32).astype(jnp.int32) >> place_in
            keep = (bits & 1).astype(F32)
            keep_next = ((bits >> 4) & 1).astype(F32)
            old = master[at, cols]
            new = old - LEARN_RATE * (
                grad[g, at, :] * scale + WEIGHT_DECAY * (1.0 - keep) * old
            )
            new_ref[at, cols] = new
            sparse_ref[at, cols] = (new * keep_next).astype(BF16)
            return carry

        lax.fori_loop(0, rows // tile, rows_of, 0)
        for store in weight_stores(g):
            store.start()

    for g in range(groups):
        grad[g] = dot(held_t[z], g_all[z, g])

    for g in range(groups):
        taken = early if g == groups - 2 else 1

        def add_gradient(i, carry):
            zp = nearest(i)

            @pl.when(i >= taken)
            def _():
                take_gradient(zp, g)

            grad[g] = grad[g] + dot(held_t[zp], g_all[zp, g])
            return carry

        if g < groups - 1:
            lax.fori_loop(1, n, add_gradient, 0)
            update(g)
            continue
        lax.fori_loop(1, 2, add_gradient, 0)
        lax.fori_loop(0, chunks, finish, 0)
        out_store = pltpu.make_async_copy(out, out_hbm, store_sem.at[0])
        out_store.start()
        lax.fori_loop(2, n, add_gradient, 0)
        update(g)

    def drain_features(i, carry):
        c, j = i // per_device, i % per_device
        for k in range(heads_axis):
            mine, _, remote = feature_parts(k, j, c)
            if k > 0:
                relay_copy(k, j, c).wait_send()

            @pl.when(jnp.logical_not(mine))
            def _():
                remote.wait_send()
        return carry

    lax.fori_loop(0, per_device * subs, drain_features, 0)

    def drain(d, carry):
        zp = (z + d) % n
        for k in range(1, heads_axis):
            share(zp, k).wait_send()
        for k in range(heads_axis):
            hand_over(zp, k, sub, 1 - sub).wait_send()

        for g in range(groups):

            @pl.when(zp > z)
            def _():
                up_copy(zp, g).wait_send()

            @pl.when(zp < z)
            def _():
                down_copy(zp, g).wait_send()

            @pl.when(jnp.logical_and(zp <= z, z < n - 1))
            def _():
                gradient_copy(zp, g, 1).wait_send()

            @pl.when(jnp.logical_and(zp >= z, z > 0))
            def _():
                gradient_copy(zp, g, 0).wait_send()
        return carry

    lax.fori_loop(0, n, drain, 0)

    def drain_chain(c, carry):
        @pl.when(z < n - 1)
        def _():
            state_copy(c).wait_send()

        @pl.when(z > 0)
        def _():
            adjoint_copy(c).wait_send()
        return carry

    lax.fori_loop(0, chunks, drain_chain, 0)
    out_store.wait()

    for g in range(groups):
        for store in weight_stores(g):
            store.wait()


def on_device(
    n, heads_axis, subs,
    hidden, inner_values, log_decay, skip_gain, cotangent, master, mask_now, mask_next,
):
    hs = heads_axis * subs
    tokens, features = hidden.shape
    rows, columns = master.shape
    width = inner_values.shape[1]
    heads = log_decay.shape[1]
    groups = columns // (2 * STATE)
    chunks = 4 * groups
    chunk_width = width // chunks
    per_device = features // rows
    scale = 2.0 / math.sqrt(features * hs)
    vmem = pl.BlockSpec(memory_space=pltpu.VMEM)
    hbm = pl.BlockSpec(memory_space=pl.ANY)
    dma = pltpu.SemaphoreType.DMA
    V = pltpu.VMEM
    return pl.pallas_call(
        functools.partial(kernel, n, heads_axis, subs, scale),
        out_shape=(
            jax.ShapeDtypeStruct((tokens, width), BF16),
            jax.ShapeDtypeStruct((rows, columns), F32),
            jax.ShapeDtypeStruct((rows, columns), BF16),
        ),
        in_specs=[hbm, hbm, hbm, vmem, pl.BlockSpec(memory_space=pltpu.SMEM), hbm, hbm, hbm],
        out_specs=(hbm, hbm, hbm),
        scratch_shapes=[
            V((tokens, width), BF16),
            V((rows, columns), F32),
            V((rows, columns), BF16),
            V((tokens, width), BF16),
            V((tokens, width), BF16),
            V((rows, columns), F32),
            V((rows // 4, columns), jnp.int32),
            V((rows // 4, columns), jnp.int32),
            V((rows, columns), BF16),
            V((rows, columns), BF16),
            V((n, tokens, rows), BF16),
            V((n, rows, tokens), BF16),
            V((groups, n, tokens, 2 * STATE), BF16),
            V((groups, n + 1, tokens, 2 * STATE), BF16),
            V((groups, tokens, 2 * STATE), F32),
            V((tokens, LANES), F32),
            V((LANES, tokens), F32),
            V((heads, tokens, tokens), F32),
            V((groups, tokens, tokens), F32),
            V((chunks, tokens, chunk_width), BF16),
            V((chunks, tokens, chunk_width), BF16),
            V((chunks, tokens, chunk_width), F32),
            V((groups, tokens, STATE), BF16),
            V((groups, tokens, STATE), BF16),
            V((groups, tokens, tokens), F32),
            V((chunks, STATE, chunk_width), F32),
            V((chunks, STATE, chunk_width), F32),
            V((chunks, STATE, chunk_width), BF16),
            V((chunks, STATE, chunk_width), BF16),
            V((chunks, STATE, chunk_width), BF16),
            V((chunks, STATE, chunk_width), BF16),
            V((groups, tokens, STATE), F32),
            V((groups, tokens, STATE), F32),
            V((n, groups, tokens, 2 * STATE), BF16),
            V((groups, rows, 2 * STATE), F32),
            V((tokens, width), F32),
            V(((heads_axis - 1) * per_device * subs, tokens // hs, rows), BF16),
            dma((5,)),
            dma((1,)),
            dma(((heads_axis - 1) * per_device * subs,)),
            dma(((heads_axis - 1) * per_device * subs,)),
            dma((per_device * hs,)),
            dma((n,)),
            dma((n * heads_axis,)),
            dma((n * heads_axis,)),
            dma((n * heads_axis,)),
            dma((n * heads_axis,)),
            dma((groups * n,)),
            dma((groups * (n + 1),)),
            dma((chunks,)),
            dma((chunks,)),
            dma((chunks,)),
            dma((chunks,)),
            dma((2 * n * groups,)),
            dma((n * groups,)),
            dma((1 + 2 * groups,)),
        ],
        compiler_params=pltpu.CompilerParams(
            collective_id=0, has_side_effects=True, vmem_limit_bytes=58 * 1024 * 1024
        ),
        name="layer_step",
    )(hidden, inner_values, cotangent, log_decay.T, skip_gain, master, mask_now, mask_next)


def solution(mesh):
    spread = P(("grp", "seq"), ("head", "sub"))
    weights = P("seq", ("head", "sub"))
    return jax.shard_map(
        functools.partial(
            on_device, mesh.shape["seq"], mesh.shape["head"], mesh.shape["sub"]
        ),
        mesh=mesh,
        in_specs=(
            spread, spread, spread, P(("head", "sub")), spread, weights, weights, weights
        ),
        out_specs=(spread, spread, spread),
        check_vma=False,
    )
```

```python
import functools
import math

import jax
import jax.numpy as jnp
from jax import lax
from jax.experimental import pallas as pl
from jax.experimental.pallas import tpu as pltpu
from jax.sharding import PartitionSpec as P

STATE = 128
LEARN_RATE = 0.05
WEIGHT_DECAY = 10.0
LANES = 128
MESH = pl.DeviceIdType.MESH
F32 = jnp.float32
BF16 = jnp.bfloat16

ROWS_FIRST = (((0,), (0,)), ((), ()))
LANES_BOTH = (((1,), (1,)), ((), ()))


def dot(a, b, dims=None):
    if dims is None:
        dims = (((1,), (0,)), ((), ()))
    return lax.dot_general(a, b, dims, preferred_element_type=F32)


def pattern_code(ids):
    code = jnp.where(ids == 0, 3.0, 12.0)
    code = jnp.where(ids == 1, 5.0, code)
    code = jnp.where(ids == 2, 9.0, code)
    code = jnp.where(ids == 3, 6.0, code)
    return jnp.where(ids == 4, 10.0, code)


def kernel(
    n, heads_axis, subs, scale,
    hid, x_in, dy_in, log_ref, skip_ref, master_in, now_in, next_in,
    out_hbm, grad_hbm, code_hbm,
    out, grad_low,
    xv, dyv, master, now, nxt, code, eff,
    held, held_t, part_out, part_in, acc,
    cum, cum_t, decay, mix_sum, xs, ys, ec, write, read, scores,
    s_loc, a_loc, s_out, a_out, s_in, a_in, g_write, g_read, g_all, grad, local,
    relay, load_sem, own_sem, send_r, recv_r, send1, recv1, send2, recv2, send3, recv3, send_p, recv_p,
    send_s, recv_s, send_a, recv_a, send_g, recv_g, store_sem,
):
    hs = heads_axis * subs
    tokens = hid.shape[0]
    part = tokens // hs
    rows, columns = master.shape
    per_device = hid.shape[1] // rows
    groups = columns // (2 * STATE)
    width = xv.shape[1]
    heads = log_ref.shape[0]
    head_width = width // heads
    in_pair = LANES // head_width
    pairs = width // LANES
    chunks, _, chunk_width = xs.shape
    chunk_pairs = chunk_width // LANES
    group_chunks = chunks // groups
    group_pairs = pairs // groups

    z = lax.axis_index("seq")
    sub = lax.axis_index("sub")
    h = lax.axis_index("head") * subs + sub
    me = z * hs + h
    upper_half = 2 * z // n
    inward = upper_half * (n - 1 - z) + (1 - upper_half) * z

    def at_least(a, b):
        return (a + 2 * n - b) // (2 * n)

    def farthest(i):
        both = 1 - at_least(i, 2 * inward)
        step = both * (i // 2) + (1 - both) * (i - inward)
        down = both * (i % 2)
        to = down * step + (1 - down) * (n - 1 - step)
        return upper_half * (n - 1 - to) + (1 - upper_half) * to

    def nearest(i):
        return farthest(n - 1 - i)

    def place(zz, hh):
        return {"seq": zz, "head": hh // subs, "sub": hh % subs}

    loads = [
        pltpu.make_async_copy(src, dst, load_sem.at[i])
        for i, (src, dst) in enumerate(
            ((x_in, xv), (dy_in, dyv), (now_in, now), (next_in, nxt), (master_in, master))
        )
    ]
    for load in loads[2:]:
        load.start()

    barrier = pltpu.get_barrier_semaphore()

    def same_line(i):
        return place(i // subs, h - sub + i % subs)

    def greet_line(i, carry):
        @pl.when(i != z * subs + sub)
        def _():
            pl.semaphore_signal(barrier, inc=1, device_id=same_line(i), device_id_type=MESH)
        return carry

    def across(k):
        return place(z, (h // subs + k) % heads_axis * subs + sub)

    for k in range(1, heads_axis):
        pl.semaphore_signal(barrier, inc=1, device_id=across(k), device_id_type=MESH)
    lax.fori_loop(0, n * subs, greet_line, 0)
    pl.semaphore_wait(barrier, n * subs - 1 + heads_axis - 1)

    def quarter(t):
        return pl.ds(pl.multiple_of(t * part, part), part)

    def plane(j):
        return pl.ds(pl.multiple_of(j * rows, rows), rows)

    def relay_copy(k, j, c):
        at = ((k - 1) * per_device + j) * subs + c
        t = (h // subs + k) % heads_axis * subs + c
        return pltpu.make_async_remote_copy(
            hid.at[quarter(t), plane(j)], relay.at[at], send_r.at[at], recv_r.at[at],
            device_id=across(k), device_id_type=MESH,
        )

    def feature_parts(k, j, c):
        t = h - sub + c
        source = ((h // subs + heads_axis - k) % heads_axis) * subs + sub
        zt = source * per_device + j
        if k == 0:
            src = hid.at[quarter(t), plane(j)]
        else:
            src = relay.at[((k - 1) * per_device + j) * subs + c]
        dst = held.at[z, quarter(t), :]
        mine = jnp.logical_and(zt == z, c == sub)
        local_copy = pltpu.make_async_copy(src, dst, own_sem.at[0])
        remote = pltpu.make_async_remote_copy(
            src, dst, send1.at[(k * per_device + j) * subs + c], recv1.at[z],
            device_id=place(zt, t), device_id_type=MESH,
        )
        return mine, local_copy, remote

    def send_features(k, j, c):
        mine, local_copy, remote = feature_parts(k, j, c)

        @pl.when(mine)
        def _():
            local_copy.start()

        @pl.when(jnp.logical_not(mine))
        def _():
            remote.start()

    def forward_features(c):
        def forward(j, carry):
            for k in range(1, heads_axis):
                relay_copy(k, j, c).wait_recv()
                send_features(k, j, c)
            return carry

        lax.fori_loop(0, per_device, forward, 0)

    def first_relays(i, carry):
        for k in range(1, heads_axis):
            relay_copy(k, i % per_device, i // per_device).start()
        return carry

    def first_sends(i, carry):
        send_features(0, i % per_device, i // per_device)
        return carry

    lax.fori_loop(0, per_device * subs, first_relays, 0)
    lax.fori_loop(0, per_device * subs, first_sends, 0)
    for load in loads[:2]:
        load.start()

    at_row = lax.broadcasted_iota(jnp.int32, (tokens, tokens), 0)
    at_lane = lax.broadcasted_iota(jnp.int32, (tokens, tokens), 1)
    upper = (at_row <= at_lane).astype(F32)
    cum_t[...] = jnp.zeros_like(cum_t)
    cum_t[:heads, :] = lax.dot_general(
        log_ref[...], upper, (((1,), (0,)), ((), ())),
        precision=lax.Precision.HIGHEST, preferred_element_type=F32,
    )
    cum[...] = cum_t[...].T

    loads[2].wait()
    loads[3].wait()
    loads[4].wait()
    small = (pattern_code(now[...]) + 16.0 * pattern_code(nxt[...])).astype(BF16)
    tile = min(rows, 128)

    def effective(i, carry):
        at = pl.ds(pl.multiple_of(i * tile, tile), tile)
        row = i * tile + lax.broadcasted_iota(jnp.int32, (tile, rows // 4), 0)
        spot = lax.broadcasted_iota(jnp.int32, (tile, rows // 4), 1)
        spread = (row // 4 == spot).astype(BF16)
        both = dot(spread, small)
        code[at, :] = both.astype(BF16)
        place_in = lax.broadcasted_iota(jnp.int32, (tile, columns), 0) % 4
        keep = ((both.astype(jnp.int32) >> place_in) & 1).astype(F32)
        eff[at, :] = (master[at, :] * keep * scale).astype(BF16)
        return carry

    lax.fori_loop(0, rows // tile, effective, 0)
    code_store = pltpu.make_async_copy(code, code_hbm, store_sem.at[1])
    code_store.start()

    loads[0].wait()
    loads[1].wait()
    mix_sum[...] = jnp.zeros_like(mix_sum)
    lane = lax.broadcasted_iota(jnp.int32, (tokens, LANES), 1)
    head_masks = [
        (lane // head_width == j).astype(BF16) for j in range(in_pair)
    ]

    def head_column(hh):
        return jnp.sum(jnp.where(lane == hh, cum[...], 0.0), axis=1, keepdims=True)

    def independent(p, carry):
        at = pl.ds(pl.multiple_of(p * LANES, LANES), LANES)
        c = p // chunk_pairs
        inner = pl.ds(pl.multiple_of((p % chunk_pairs) * LANES, LANES), LANES)
        x2, d2 = xv[:, at], dyv[:, at]
        total = jnp.zeros((tokens, tokens), F32)
        across = jnp.zeros((tokens, LANES), F32)
        for j in range(in_pair):
            hh = p * in_pair + j
            column = head_column(hh)
            across = jnp.where(lane // head_width == j, column, across)
            spread = column - cum_t[pl.ds(hh, 1), :]
            factor = jnp.exp(jnp.where(at_row >= at_lane, spread, -1e30))
            decay[hh] = factor
            total = total + dot(d2 * head_masks[j], x2, LANES_BOTH) * factor
        g = p // group_pairs
        mix_sum[g] = mix_sum[g] + total
        grown = jnp.exp(across)
        left = jnp.exp(across[tokens - 1 :, :] - across)
        ec[c, :, inner] = grown
        xs[c, :, inner] = (x2.astype(F32) * left).astype(BF16)
        ys[c, :, inner] = (d2.astype(F32) * grown).astype(BF16)
        return carry

    from_h = z // per_device

    def share(zp, k):
        head = (h // subs + k) % heads_axis
        return pltpu.make_async_remote_copy(
            held.at[zp, quarter(h), :], held.at[zp, quarter(h), :],
            send2.at[zp * heads_axis + k], recv2.at[zp * heads_axis + k],
            device_id=place(z, head * subs + sub), device_id_type=MESH,
        )

    def shared(zp, k):
        t = ((h // subs + heads_axis - k) % heads_axis) * subs + sub
        return pltpu.make_async_remote_copy(
            held.at[zp, quarter(t), :], held.at[zp, quarter(t), :],
            send2.at[zp * heads_axis + k], recv2.at[zp * heads_axis + k],
            device_id=place(z, t), device_id_type=MESH,
        )

    def hand_over(zp, k, from_sub, to_sub):
        t = ((h // subs + heads_axis - k) % heads_axis) * subs + from_sub
        return pltpu.make_async_remote_copy(
            held.at[zp, quarter(t), :], held.at[zp, quarter(t), :],
            send3.at[zp * heads_axis + k], recv3.at[zp * heads_axis + k],
            device_id=place(z, h - sub + to_sub), device_id_type=MESH,
        )

    outer = at_least(inward, 1)
    skipped = outer * (2 * inward - 1) + (1 - outer) * (n - 2)

    def token_block(d):
        i = d - 2
        far = farthest(i + at_least(i, skipped))
        own = 1 - at_least(d, 1)
        first = at_least(d, 1) * (1 - at_least(d, 2))
        return own * z + first * farthest(skipped) + at_least(d, 2) * far

    def arrived(d):
        zp = token_block(d)
        mine = jnp.logical_and(zp == z, from_h % subs == sub)

        @pl.when(mine)
        def _():
            pltpu.make_async_copy(
                held.at[zp, quarter(h), :], held.at[zp, quarter(h), :], own_sem.at[0]
            ).wait()

        @pl.when(jnp.logical_not(mine))
        def _():
            pltpu.make_async_remote_copy(
                held.at[zp, quarter(h), :], held.at[zp, quarter(h), :],
                send1.at[0], recv1.at[zp],
                device_id=place(z, h - sub + 1 - sub), device_id_type=MESH,
            ).wait_recv()

        for k in range(1, heads_axis):
            share(zp, k).start()
        hand_over(zp, 0, sub, 1 - sub).start()

    def crossed(d):
        zp = token_block(d)
        for k in range(1, heads_axis):
            shared(zp, k).wait_recv()
            hand_over(zp, k, sub, 1 - sub).start()

    for c in range(subs):
        forward_features(c)
    arrived(0)
    lax.fori_loop(0, pairs // 2, independent, 0)
    arrived(1)
    crossed(0)
    lax.fori_loop(pairs // 2, pairs, independent, 0)
    arrived(2)


    def merges(zs, t):
        up = at_least(t, zs)
        return up * (zs % 2) + (1 - up) * ((n - 1 - zs) % 2)

    def part_copy(t, g):
        merged = merges(z, t)
        to = merged * t + (1 - merged) * (z + 2 * at_least(t, z) - 1)
        final = at_least(t, to) * at_least(to, t)
        slot = final * (n + z) + (1 - final) * t
        return pltpu.make_async_remote_copy(
            part_out.at[g, t], part_in.at[g, slot],
            send_p.at[g * n + t], recv_p.at[g * 2 * n + slot],
            device_id=place(to, h), device_id_type=MESH,
        )

    def part_arrival(slot, g):
        pltpu.make_async_remote_copy(
            part_in.at[g, slot], part_in.at[g, slot],
            send_p.at[0], recv_p.at[g * 2 * n + slot],
            device_id=across(1), device_id_type=MESH,
        ).wait_recv()

    def own_product(g):
        acc[g] = dot(held[z], eff[:, g * 2 * STATE : (g + 1) * 2 * STATE])

    def product(t, g):
        result = dot(held[t], eff[:, g * 2 * STATE : (g + 1) * 2 * STATE])
        merged = merges(z, t)

        @pl.when(merged == 0)
        def _():
            part_out[g, t] = result.astype(BF16)

        @pl.when(merged == 1)
        def _():
            part_arrival(t, g)
            part_out[g, t] = (result + part_in[g, t].astype(F32)).astype(BF16)

        part_copy(t, g).start()

    def ready(d):
        zp = token_block(d)
        for k in range(heads_axis):
            hand_over(zp, k, 1 - sub, sub).wait_recv()
        return zp

    crossed(1)
    ready(0)
    for g in range(groups):
        own_product(g)

    def project(d, carry):
        @pl.when(d + 1 < n)
        def _():
            arrived(d + 1)

        product(ready(d - 1), 0)
        crossed(d)
        return carry

    lax.fori_loop(2, n, project, 0)
    product(ready(n - 1), 0)
    for g in range(1, groups):

        def later_product(d, carry):
            product(token_block(d), g)
            return carry

        lax.fori_loop(2, n, later_product, 0)
        product(token_block(1), g)

    def turn(zp, carry):
        held_t[zp] = held[zp].T
        return carry

    lax.fori_loop(0, n, turn, 0)

    def state_copy(c):
        return pltpu.make_async_remote_copy(
            s_out.at[c], s_in.at[c], send_s.at[c], recv_s.at[c],
            device_id=place(lax.rem(z + 1, n), h), device_id_type=MESH,
        )

    def adjoint_copy(c):
        return pltpu.make_async_remote_copy(
            a_out.at[c], a_in.at[c], send_a.at[c], recv_a.at[c],
            device_id=place(lax.rem(z + n - 1, n), h), device_id_type=MESH,
        )

    def block_states(c, carry):
        g = c // group_chunks
        state = dot(write[g], xs[c], ROWS_FIRST)
        adjoint = dot(read[g], ys[c], ROWS_FIRST)
        s_loc[c] = state
        a_loc[c] = adjoint

        @pl.when(z == 0)
        def _():
            s_in[c] = jnp.zeros_like(s_in[c])
            s_out[c] = state.astype(BF16)
            state_copy(c).start()

        @pl.when(z == n - 1)
        def _():
            a_in[c] = jnp.zeros_like(a_in[c])
            a_out[c] = adjoint.astype(BF16)
            adjoint_copy(c).start()
        return carry

    def mixing(p, carry):
        at = pl.ds(pl.multiple_of(p * LANES, LANES), LANES)
        x2 = xv[:, at]
        g = p // group_pairs
        gain = jnp.zeros((tokens, LANES), F32)
        result = jnp.zeros((tokens, LANES), F32)
        for j in range(in_pair):
            hh = p * in_pair + j
            gain = jnp.where(lane // head_width == j, skip_ref[hh], gain)
            mix = (scores[g] * decay[hh]).astype(BF16)
            result = result + dot(mix, x2 * head_masks[j])
        local[:, at] = result + gain * x2.astype(F32)
        return carry

    def pass_state(c):
        @pl.when(z > 0)
        def _():
            state_copy(c).wait_recv()

            @pl.when(z < n - 1)
            def _():
                end = ec[c, tokens - 1 :, :]
                s_out[c] = (end * s_in[c].astype(F32) + s_loc[c]).astype(BF16)
                state_copy(c).start()

    def pass_adjoint(c):
        @pl.when(z < n - 1)
        def _():
            adjoint_copy(c).wait_recv()

            @pl.when(z > 0)
            def _():
                end = ec[c, tokens - 1 :, :]
                a_out[c] = (end * a_in[c].astype(F32) + a_loc[c]).astype(BF16)
                adjoint_copy(c).start()

    def gradient_copy(zp, g, kind, up):
        to = z + 1 if up else z - 1
        at = (zp * groups + g) * 2 + kind
        cols = pl.ds(pl.multiple_of(kind * STATE, STATE), STATE)
        return pltpu.make_async_remote_copy(
            g_all.at[zp, g, :, cols], g_all.at[zp, g, :, cols],
            send_g.at[up * 2 * n * groups + at], recv_g.at[at],
            device_id=place(to, h), device_id_type=MESH,
        )

    def pass_gradient(zp, g, kind):
        @pl.when(jnp.logical_and(zp <= z, z < n - 1))
        def _():
            gradient_copy(zp, g, kind, 1).start()

        @pl.when(jnp.logical_and(zp >= z, z > 0))
        def _():
            gradient_copy(zp, g, kind, 0).start()

    def take_gradient(zp, g, second):
        upper = 2 * zp // n
        kind = second * upper + (1 - second) * (1 - upper)
        at = (zp * groups + g) * 2 + kind
        cols = pl.ds(pl.multiple_of(kind * STATE, STATE), STATE)
        pltpu.make_async_remote_copy(
            g_all.at[zp, g, :, cols], g_all.at[zp, g, :, cols],
            send_g.at[0], recv_g.at[at],
            device_id=across(1), device_id_type=MESH,
        ).wait_recv()
        pass_gradient(zp, g, kind)

    between = jnp.logical_and(z > 0, z < n - 1)

    def take_near(g, second):
        take_gradient(nearest(1), g, second)

        @pl.when(between)
        def _():
            take_gradient(nearest(2), g, second)

    def take_far(g, second):
        def take(i, carry):
            @pl.when(jnp.logical_not(jnp.logical_and(between, i == 2)))
            def _():
                take_gradient(nearest(i), g, second)
            return carry

        lax.fori_loop(2, n, take, 0)

    def state_end(c, g):
        pass_state(c)
        g_read[g] = g_read[g] + dot(ys[c], s_in[c], LANES_BOTH)

    def adjoint_end(c, g):
        pass_adjoint(c)
        g_write[g] = g_write[g] + dot(xs[c], a_in[c], LANES_BOTH)

    def chain_end(c, g, second):
        @pl.when((2 * z < n) != second)
        def _():
            state_end(c, g)

        @pl.when((2 * z < n) == second)
        def _():
            adjoint_end(c, g)

    def send_gradient(g, second):
        @pl.when((2 * z < n) != second)
        def _():
            g_all[z, g, :, STATE:] = g_read[g].astype(BF16)
            pass_gradient(z, g, 1)

        @pl.when((2 * z < n) == second)
        def _():
            g_all[z, g, :, :STATE] = g_write[g].astype(BF16)
            pass_gradient(z, g, 0)

    def begin(g):
        def collect(zs, carry):
            adjacent = at_least(zs + 1, z) * at_least(z + 1, zs)

            @pl.when(jnp.logical_and(zs != z, merges(zs, z) + adjacent > 0))
            def _():
                part_arrival(n + zs, g)
                acc[g] = acc[g] + part_in[g, n + zs].astype(F32)
            return carry

        lax.fori_loop(0, n, collect, 0)
        write[g] = acc[g, :, :STATE].astype(BF16)
        read[g] = acc[g, :, STATE:].astype(BF16)
        lax.fori_loop(g * group_chunks, (g + 1) * group_chunks, block_states, 0)
        scores[g] = dot(read[g], write[g], LANES_BOTH)
        mixed = mix_sum[g].astype(BF16)
        g_write[g] = dot(mixed, read[g], ROWS_FIRST)
        g_read[g] = dot(mixed, write[g])

    begin(0)
    ahead = group_chunks // 2
    for g in range(groups + 1):

        def chain(i, carry):
            if g > 0:
                before = (g - 1) * group_chunks + i

                @pl.when(jnp.logical_not(jnp.logical_and(between, i < ahead)))
                def _():
                    chain_end(before, g - 1, True)

            if g < groups:
                c = g * group_chunks + i
                chain_end(c, g, False)
                lax.fori_loop(c * chunk_pairs, (c + 1) * chunk_pairs, mixing, 0)
            return carry

        lax.fori_loop(0, group_chunks, chain, 0)
        if g > 0:
            send_gradient(g - 1, True)
        if g < groups:
            send_gradient(g, False)

            @pl.when(between)
            def _():
                def chain_ahead(c, carry):
                    chain_end(c, g, True)
                    return carry

                lax.fori_loop(g * group_chunks, g * group_chunks + ahead, chain_ahead, 0)

        if g + 1 < groups:
            begin(g + 1)
        if g > 0 and g < groups:
            take_near(g - 1, 0)

    def finish(c, carry):
        at = pl.ds(pl.multiple_of(c * chunk_width, chunk_width), chunk_width)
        carried = dot(read[c // group_chunks], s_in[c])
        out[:, at] = (local[:, at] + ec[c] * carried).astype(BF16)
        return carry

    def gradient_store(g):
        cols = pl.ds(g * 2 * STATE, 2 * STATE)
        return pltpu.make_async_copy(
            grad_low.at[:, cols], grad_hbm.at[:, cols], store_sem.at[2 + g]
        )

    def keep_gradient(g):
        grad_low[:, g * 2 * STATE : (g + 1) * 2 * STATE] = grad[g].astype(BF16)
        gradient_store(g).start()

    def own_terms(g):
        grad[g] = dot(held_t[z], g_all[z, g])

    def add_terms(first, g):
        def add(i, carry):
            zp = nearest(i)
            grad[g] = grad[g] + dot(held_t[zp], g_all[zp, g])
            return carry

        lax.fori_loop(first, n, add, 0)

    last = groups - 1
    for g in range(last):
        take_far(g, 0)
        take_near(g, 1)
    take_near(last, 0)
    lax.fori_loop(0, chunks, finish, 0)
    out_store = pltpu.make_async_copy(out, out_hbm, store_sem.at[0])
    out_store.start()
    for g in range(last):
        take_far(g, 1)
    take_far(last, 0)
    take_near(last, 1)
    for g in range(last):
        own_terms(g)
        add_terms(1, g)
        keep_gradient(g)
    take_far(last, 1)
    own_terms(last)
    add_terms(1, last)
    keep_gradient(last)

    def drain_features(i, carry):
        c, j = i // per_device, i % per_device
        for k in range(heads_axis):
            mine, _, remote = feature_parts(k, j, c)
            if k > 0:
                relay_copy(k, j, c).wait_send()

            @pl.when(jnp.logical_not(mine))
            def _():
                remote.wait_send()
        return carry

    lax.fori_loop(0, per_device * subs, drain_features, 0)

    def drain(d, carry):
        zp = (z + d) % n
        for k in range(1, heads_axis):
            share(zp, k).wait_send()
        for k in range(heads_axis):
            hand_over(zp, k, sub, 1 - sub).wait_send()

        for g in range(groups):

            @pl.when(zp != z)
            def _():
                part_copy(zp, g).wait_send()

            for kind in range(2):

                @pl.when(jnp.logical_and(zp <= z, z < n - 1))
                def _():
                    gradient_copy(zp, g, kind, 1).wait_send()

                @pl.when(jnp.logical_and(zp >= z, z > 0))
                def _():
                    gradient_copy(zp, g, kind, 0).wait_send()
        return carry

    lax.fori_loop(0, n, drain, 0)

    def drain_chain(c, carry):
        @pl.when(z < n - 1)
        def _():
            state_copy(c).wait_send()

        @pl.when(z > 0)
        def _():
            adjoint_copy(c).wait_send()
        return carry

    lax.fori_loop(0, chunks, drain_chain, 0)
    out_store.wait()

    code_store.wait()
    for g in range(groups):
        gradient_store(g).wait()


def update(scale, master, code, grad, out_in, new_ref, sparse_ref, out):
    place_in = lax.broadcasted_iota(jnp.int32, master.shape, 0) % 4
    bits = code[...].astype(F32).astype(jnp.int32) >> place_in
    keep = (bits & 1).astype(F32)
    keep_next = ((bits >> 4) & 1).astype(F32)
    old = master[...]
    new = old - LEARN_RATE * (
        grad[...].astype(F32) * scale + WEIGHT_DECAY * (1.0 - keep) * old
    )
    new_ref[...] = new
    sparse_ref[...] = (new * keep_next).astype(BF16)
    out[...] = out_in[...]


def on_device(
    n, heads_axis, subs,
    hidden, inner_values, log_decay, skip_gain, cotangent, master, mask_now, mask_next,
):
    hs = heads_axis * subs
    tokens, features = hidden.shape
    rows, columns = master.shape
    width = inner_values.shape[1]
    heads = log_decay.shape[1]
    groups = columns // (2 * STATE)
    chunks = 4 * groups
    chunk_width = width // chunks
    per_device = features // rows
    scale = 2.0 / math.sqrt(features * hs)
    vmem = pl.BlockSpec(memory_space=pltpu.VMEM)
    hbm = pl.BlockSpec(memory_space=pl.ANY)
    dma = pltpu.SemaphoreType.DMA
    V = pltpu.VMEM
    out, grad, code = pl.pallas_call(
        functools.partial(kernel, n, heads_axis, subs, scale),
        out_shape=(
            jax.ShapeDtypeStruct((tokens, width), BF16),
            jax.ShapeDtypeStruct((rows, columns), BF16),
            jax.ShapeDtypeStruct((rows, columns), BF16),
        ),
        in_specs=[hbm, hbm, hbm, vmem, pl.BlockSpec(memory_space=pltpu.SMEM), hbm, hbm, hbm],
        out_specs=(hbm, hbm, hbm),
        scratch_shapes=[
            V((tokens, width), BF16),
            V((rows, columns), BF16),
            V((tokens, width), BF16),
            V((tokens, width), BF16),
            V((rows, columns), F32),
            V((rows // 4, columns), jnp.int32),
            V((rows // 4, columns), jnp.int32),
            V((rows, columns), BF16),
            V((rows, columns), BF16),
            V((n, tokens, rows), BF16),
            V((n, rows, tokens), BF16),
            V((groups, n, tokens, 2 * STATE), BF16),
            V((groups, 2 * n, tokens, 2 * STATE), BF16),
            V((groups, tokens, 2 * STATE), F32),
            V((tokens, LANES), F32),
            V((LANES, tokens), F32),
            V((heads, tokens, tokens), F32),
            V((groups, tokens, tokens), F32),
            V((chunks, tokens, chunk_width), BF16),
            V((chunks, tokens, chunk_width), BF16),
            V((chunks, tokens, chunk_width), F32),
            V((groups, tokens, STATE), BF16),
            V((groups, tokens, STATE), BF16),
            V((groups, tokens, tokens), F32),
            V((chunks, STATE, chunk_width), F32),
            V((chunks, STATE, chunk_width), F32),
            V((chunks, STATE, chunk_width), BF16),
            V((chunks, STATE, chunk_width), BF16),
            V((chunks, STATE, chunk_width), BF16),
            V((chunks, STATE, chunk_width), BF16),
            V((groups, tokens, STATE), F32),
            V((groups, tokens, STATE), F32),
            V((n, groups, tokens, 2 * STATE), BF16),
            V((groups, rows, 2 * STATE), F32),
            V((tokens, width), F32),
            V(((heads_axis - 1) * per_device * subs, tokens // hs, rows), BF16),
            dma((5,)),
            dma((1,)),
            dma(((heads_axis - 1) * per_device * subs,)),
            dma(((heads_axis - 1) * per_device * subs,)),
            dma((per_device * hs,)),
            dma((n,)),
            dma((n * heads_axis,)),
            dma((n * heads_axis,)),
            dma((n * heads_axis,)),
            dma((n * heads_axis,)),
            dma((groups * n,)),
            dma((groups * 2 * n,)),
            dma((chunks,)),
            dma((chunks,)),
            dma((chunks,)),
            dma((chunks,)),
            dma((4 * n * groups,)),
            dma((2 * n * groups,)),
            dma((2 + groups,)),
        ],
        compiler_params=pltpu.CompilerParams(
            collective_id=0, has_side_effects=True, vmem_limit_bytes=58 * 1024 * 1024
        ),
        name="layer_step",
    )(hidden, inner_values, cotangent, log_decay.T, skip_gain, master, mask_now, mask_next)
    steps = 2
    weights = pl.BlockSpec((rows // steps, columns), lambda i: (i, 0))
    positions = pl.BlockSpec((tokens // steps, width), lambda i: (i, 0))
    new, sparse, out = pl.pallas_call(
        functools.partial(update, scale),
        grid=(steps,),
        out_shape=(
            jax.ShapeDtypeStruct((rows, columns), F32),
            jax.ShapeDtypeStruct((rows, columns), BF16),
            jax.ShapeDtypeStruct((tokens, width), BF16),
        ),
        in_specs=[weights, weights, weights, positions],
        out_specs=(weights, weights, positions),
        compiler_params=pltpu.CompilerParams(vmem_limit_bytes=58 * 1024 * 1024),
        name="weight_update",
    )(master, code, grad, out)
    return out, new, sparse


def solution(mesh):
    spread = P(("grp", "seq"), ("head", "sub"))
    weights = P("seq", ("head", "sub"))
    return jax.shard_map(
        functools.partial(
            on_device, mesh.shape["seq"], mesh.shape["head"], mesh.shape["sub"]
        ),
        mesh=mesh,
        in_specs=(
            spread, spread, spread, P(("head", "sub")), spread, weights, weights, weights
        ),
        out_specs=(spread, spread, spread),
        check_vma=False,
    )
```

```python
import functools
import math

import jax
import jax.numpy as jnp
from jax import lax
from jax.experimental import pallas as pl
from jax.experimental.pallas import tpu as pltpu
from jax.sharding import PartitionSpec as P

STATE = 128
LEARN_RATE = 0.05
WEIGHT_DECAY = 10.0
LANES = 128
MESH = pl.DeviceIdType.MESH
F32 = jnp.float32
BF16 = jnp.bfloat16

ROWS_FIRST = (((0,), (0,)), ((), ()))
LANES_BOTH = (((1,), (1,)), ((), ()))


def dot(a, b, dims=None):
    if dims is None:
        dims = (((1,), (0,)), ((), ()))
    return lax.dot_general(a, b, dims, preferred_element_type=F32)


def pattern_code(ids):
    code = jnp.where(ids == 0, 3.0, 12.0)
    code = jnp.where(ids == 1, 5.0, code)
    code = jnp.where(ids == 2, 9.0, code)
    code = jnp.where(ids == 3, 6.0, code)
    return jnp.where(ids == 4, 10.0, code)


def kernel(
    n, heads_axis, subs, scale,
    hid, x_in, dy_in, log_ref, skip_ref, master_in, now_in, next_in,
    out_hbm, grad_hbm, code_hbm,
    out, grad_low,
    xv, dyv, master, now, nxt, code, eff,
    held, held_t, part_out, part_in, acc,
    cum, cum_t, decay, mix_sum, xs, ys, ec, write, read, scores,
    s_loc, a_loc, s_out, a_out, s_in, a_in, g_write, g_read, g_all, grad, local,
    relay, load_sem, own_sem, send_r, recv_r, send1, recv1, send2, recv2, send3, recv3, send_p, recv_p,
    send_s, recv_s, send_a, recv_a, send_g, recv_g, store_sem,
):
    hs = heads_axis * subs
    tokens = hid.shape[0]
    part = tokens // hs
    rows, columns = master.shape
    per_device = hid.shape[1] // rows
    groups = columns // (2 * STATE)
    width = xv.shape[1]
    heads = log_ref.shape[0]
    head_width = width // heads
    in_pair = LANES // head_width
    pairs = width // LANES
    chunks, _, chunk_width = xs.shape
    chunk_pairs = chunk_width // LANES
    group_chunks = chunks // groups
    group_pairs = pairs // groups

    z = lax.axis_index("seq")
    sub = lax.axis_index("sub")
    h = lax.axis_index("head") * subs + sub
    me = z * hs + h
    upper_half = 2 * z // n
    inward = upper_half * (n - 1 - z) + (1 - upper_half) * z

    def at_least(a, b):
        return (a + 2 * n - b) // (2 * n)

    def farthest(i):
        both = 1 - at_least(i, 2 * inward)
        step = both * (i // 2) + (1 - both) * (i - inward)
        down = both * (i % 2)
        to = down * step + (1 - down) * (n - 1 - step)
        return upper_half * (n - 1 - to) + (1 - upper_half) * to

    def nearest(i):
        return farthest(n - 1 - i)

    def place(zz, hh):
        return {"seq": zz, "head": hh // subs, "sub": hh % subs}

    loads = [
        pltpu.make_async_copy(src, dst, load_sem.at[i])
        for i, (src, dst) in enumerate(
            ((x_in, xv), (dy_in, dyv), (now_in, now), (next_in, nxt), (master_in, master))
        )
    ]
    for load in loads[2:]:
        load.start()

    barrier = pltpu.get_barrier_semaphore()

    def same_line(i):
        return place(i // subs, h - sub + i % subs)

    def greet_line(i, carry):
        @pl.when(i != z * subs + sub)
        def _():
            pl.semaphore_signal(barrier, inc=1, device_id=same_line(i), device_id_type=MESH)
        return carry

    def across(k):
        return place(z, (h // subs + k) % heads_axis * subs + sub)

    for k in range(1, heads_axis):
        pl.semaphore_signal(barrier, inc=1, device_id=across(k), device_id_type=MESH)
    lax.fori_loop(0, n * subs, greet_line, 0)
    pl.semaphore_wait(barrier, n * subs - 1 + heads_axis - 1)

    def quarter(t):
        return pl.ds(pl.multiple_of(t * part, part), part)

    def plane(j):
        return pl.ds(pl.multiple_of(j * rows, rows), rows)

    def relay_copy(k, j, c):
        at = ((k - 1) * per_device + j) * subs + c
        t = (h // subs + k) % heads_axis * subs + c
        return pltpu.make_async_remote_copy(
            hid.at[quarter(t), plane(j)], relay.at[at], send_r.at[at], recv_r.at[at],
            device_id=across(k), device_id_type=MESH,
        )

    def feature_parts(k, j, c):
        t = h - sub + c
        source = ((h // subs + heads_axis - k) % heads_axis) * subs + sub
        zt = source * per_device + j
        if k == 0:
            src = hid.at[quarter(t), plane(j)]
        else:
            src = relay.at[((k - 1) * per_device + j) * subs + c]
        dst = held.at[z, quarter(t), :]
        mine = jnp.logical_and(zt == z, c == sub)
        local_copy = pltpu.make_async_copy(src, dst, own_sem.at[0])
        remote = pltpu.make_async_remote_copy(
            src, dst, send1.at[(k * per_device + j) * subs + c], recv1.at[z],
            device_id=place(zt, t), device_id_type=MESH,
        )
        return mine, local_copy, remote

    def send_features(k, j, c):
        mine, local_copy, remote = feature_parts(k, j, c)

        @pl.when(mine)
        def _():
            local_copy.start()

        @pl.when(jnp.logical_not(mine))
        def _():
            remote.start()

    def forward_features(c):
        def forward(j, carry):
            for k in range(1, heads_axis):
                relay_copy(k, j, c).wait_recv()
                send_features(k, j, c)
            return carry

        lax.fori_loop(0, per_device, forward, 0)

    def first_relays(i, carry):
        for k in range(1, heads_axis):
            relay_copy(k, i % per_device, i // per_device).start()
        return carry

    def first_sends(i, carry):
        send_features(0, i % per_device, i // per_device)
        return carry

    lax.fori_loop(0, per_device * subs, first_relays, 0)
    lax.fori_loop(0, per_device * subs, first_sends, 0)
    for load in loads[:2]:
        load.start()

    at_row = lax.broadcasted_iota(jnp.int32, (tokens, tokens), 0)
    at_lane = lax.broadcasted_iota(jnp.int32, (tokens, tokens), 1)
    upper = (at_row <= at_lane).astype(F32)
    cum_t[...] = jnp.zeros_like(cum_t)
    cum_t[:heads, :] = lax.dot_general(
        log_ref[...], upper, (((1,), (0,)), ((), ())),
        precision=lax.Precision.HIGHEST, preferred_element_type=F32,
    )
    cum[...] = cum_t[...].T

    loads[2].wait()
    loads[3].wait()
    loads[4].wait()
    small = (pattern_code(now[...]) + 16.0 * pattern_code(nxt[...])).astype(BF16)
    tile = min(rows, 128)

    def effective(i, carry):
        at = pl.ds(pl.multiple_of(i * tile, tile), tile)
        row = i * tile + lax.broadcasted_iota(jnp.int32, (tile, rows // 4), 0)
        spot = lax.broadcasted_iota(jnp.int32, (tile, rows // 4), 1)
        spread = (row // 4 == spot).astype(BF16)
        both = dot(spread, small)
        code[at, :] = both.astype(BF16)
        place_in = lax.broadcasted_iota(jnp.int32, (tile, columns), 0) % 4
        keep = ((both.astype(jnp.int32) >> place_in) & 1).astype(F32)
        eff[at, :] = (master[at, :] * keep * scale).astype(BF16)
        return carry

    lax.fori_loop(0, rows // tile, effective, 0)
    code_store = pltpu.make_async_copy(code, code_hbm, store_sem.at[1])
    code_store.start()

    loads[0].wait()
    loads[1].wait()
    mix_sum[...] = jnp.zeros_like(mix_sum)
    lane = lax.broadcasted_iota(jnp.int32, (tokens, LANES), 1)
    head_masks = [
        (lane // head_width == j).astype(BF16) for j in range(in_pair)
    ]

    def head_column(hh):
        return jnp.sum(jnp.where(lane == hh, cum[...], 0.0), axis=1, keepdims=True)

    def independent(p, carry):
        at = pl.ds(pl.multiple_of(p * LANES, LANES), LANES)
        c = p // chunk_pairs
        inner = pl.ds(pl.multiple_of((p % chunk_pairs) * LANES, LANES), LANES)
        x2, d2 = xv[:, at], dyv[:, at]
        total = jnp.zeros((tokens, tokens), F32)
        across = jnp.zeros((tokens, LANES), F32)
        for j in range(in_pair):
            hh = p * in_pair + j
            column = head_column(hh)
            across = jnp.where(lane // head_width == j, column, across)
            spread = column - cum_t[pl.ds(hh, 1), :]
            factor = jnp.exp(jnp.where(at_row >= at_lane, spread, -1e30))
            decay[hh] = factor
            total = total + dot(d2 * head_masks[j], x2, LANES_BOTH) * factor
        g = p // group_pairs
        mix_sum[g] = mix_sum[g] + total
        grown = jnp.exp(across)
        left = jnp.exp(across[tokens - 1 :, :] - across)
        ec[c, :, inner] = grown
        xs[c, :, inner] = (x2.astype(F32) * left).astype(BF16)
        ys[c, :, inner] = (d2.astype(F32) * grown).astype(BF16)
        return carry

    from_h = z // per_device
    between = jnp.logical_and(z > 0, z < n - 1)

    def share(zp, k):
        head = (h // subs + k) % heads_axis
        return pltpu.make_async_remote_copy(
            held.at[zp, quarter(h), :], held.at[zp, quarter(h), :],
            send2.at[zp * heads_axis + k], recv2.at[zp * heads_axis + k],
            device_id=place(z, head * subs + sub), device_id_type=MESH,
        )

    def shared(zp, k):
        t = ((h // subs + heads_axis - k) % heads_axis) * subs + sub
        return pltpu.make_async_remote_copy(
            held.at[zp, quarter(t), :], held.at[zp, quarter(t), :],
            send2.at[zp * heads_axis + k], recv2.at[zp * heads_axis + k],
            device_id=place(z, t), device_id_type=MESH,
        )

    def hand_over(zp, k, from_sub, to_sub):
        t = ((h // subs + heads_axis - k) % heads_axis) * subs + from_sub
        return pltpu.make_async_remote_copy(
            held.at[zp, quarter(t), :], held.at[zp, quarter(t), :],
            send3.at[zp * heads_axis + k], recv3.at[zp * heads_axis + k],
            device_id=place(z, h - sub + to_sub), device_id_type=MESH,
        )

    outer = at_least(inward, 1)
    skipped = outer * (2 * inward - 1) + (1 - outer) * (n - 2)

    def token_block(d):
        i = d - 2
        far = farthest(i + at_least(i, skipped))
        own = 1 - at_least(d, 1)
        first = at_least(d, 1) * (1 - at_least(d, 2))
        return own * z + first * farthest(skipped) + at_least(d, 2) * far

    def arrived(d):
        zp = token_block(d)
        mine = jnp.logical_and(zp == z, from_h % subs == sub)

        @pl.when(mine)
        def _():
            pltpu.make_async_copy(
                held.at[zp, quarter(h), :], held.at[zp, quarter(h), :], own_sem.at[0]
            ).wait()

        @pl.when(jnp.logical_not(mine))
        def _():
            pltpu.make_async_remote_copy(
                held.at[zp, quarter(h), :], held.at[zp, quarter(h), :],
                send1.at[0], recv1.at[zp],
                device_id=place(z, h - sub + 1 - sub), device_id_type=MESH,
            ).wait_recv()

        for k in range(1, heads_axis):
            share(zp, k).start()
        hand_over(zp, 0, sub, 1 - sub).start()

    def crossed(d):
        zp = token_block(d)
        for k in range(1, heads_axis):
            shared(zp, k).wait_recv()
            hand_over(zp, k, sub, 1 - sub).start()

    for c in range(subs):
        forward_features(c)
    arrived(0)
    lax.fori_loop(0, pairs // 2, independent, 0)
    arrived(1)
    crossed(0)
    lax.fori_loop(pairs // 2, pairs, independent, 0)
    arrived(2)


    def merges(zs, t):
        up = at_least(t, zs)
        return up * (zs % 2) + (1 - up) * ((n - 1 - zs) % 2)

    def part_copy(t, g):
        merged = merges(z, t)
        to = merged * t + (1 - merged) * (z + 2 * at_least(t, z) - 1)
        final = at_least(t, to) * at_least(to, t)
        slot = final * (n + z) + (1 - final) * t
        return pltpu.make_async_remote_copy(
            part_out.at[g, t], part_in.at[g, slot],
            send_p.at[g * n + t], recv_p.at[g * 2 * n + slot],
            device_id=place(to, h), device_id_type=MESH,
        )

    def part_arrival(slot, g):
        pltpu.make_async_remote_copy(
            part_in.at[g, slot], part_in.at[g, slot],
            send_p.at[0], recv_p.at[g * 2 * n + slot],
            device_id=across(1), device_id_type=MESH,
        ).wait_recv()

    def own_product(g):
        acc[g] = dot(held[z], eff[:, g * 2 * STATE : (g + 1) * 2 * STATE])

    def product(t, g):
        result = dot(held[t], eff[:, g * 2 * STATE : (g + 1) * 2 * STATE])
        merged = merges(z, t)

        @pl.when(merged == 0)
        def _():
            part_out[g, t] = result.astype(BF16)

        @pl.when(merged == 1)
        def _():
            part_arrival(t, g)
            part_out[g, t] = (result + part_in[g, t].astype(F32)).astype(BF16)

        part_copy(t, g).start()

    def ready(d):
        zp = token_block(d)
        for k in range(heads_axis):
            hand_over(zp, k, 1 - sub, sub).wait_recv()
        return zp

    crossed(1)
    ready(0)
    for g in range(groups):
        own_product(g)

    def project(d, carry):
        @pl.when(d + 1 < n)
        def _():
            arrived(d + 1)

        product(ready(d - 1), 0)
        crossed(d)
        return carry

    lax.fori_loop(2, n, project, 0)
    product(ready(n - 1), 0)
    for g in range(1, groups):

        def later_product(d, carry):
            product(token_block(d), g)
            return carry

        lax.fori_loop(2, n, later_product, 0)

        @pl.when(between)
        def _():
            product(token_block(1), g)


    def turn(zp, carry):
        held_t[zp] = held[zp].T
        return carry

    lax.fori_loop(0, n, turn, 0)

    def state_copy(c):
        return pltpu.make_async_remote_copy(
            s_out.at[c], s_in.at[c], send_s.at[c], recv_s.at[c],
            device_id=place(lax.rem(z + 1, n), h), device_id_type=MESH,
        )

    def adjoint_copy(c):
        return pltpu.make_async_remote_copy(
            a_out.at[c], a_in.at[c], send_a.at[c], recv_a.at[c],
            device_id=place(lax.rem(z + n - 1, n), h), device_id_type=MESH,
        )

    def block_states(c, carry):
        g = c // group_chunks
        state = dot(write[g], xs[c], ROWS_FIRST)
        adjoint = dot(read[g], ys[c], ROWS_FIRST)
        s_loc[c] = state
        a_loc[c] = adjoint

        @pl.when(z == 0)
        def _():
            s_in[c] = jnp.zeros_like(s_in[c])
            s_out[c] = state.astype(BF16)
            state_copy(c).start()

        @pl.when(z == n - 1)
        def _():
            a_in[c] = jnp.zeros_like(a_in[c])
            a_out[c] = adjoint.astype(BF16)
            adjoint_copy(c).start()
        return carry

    def mixing(p, carry):
        at = pl.ds(pl.multiple_of(p * LANES, LANES), LANES)
        x2 = xv[:, at]
        g = p // group_pairs
        gain = jnp.zeros((tokens, LANES), F32)
        result = jnp.zeros((tokens, LANES), F32)
        for j in range(in_pair):
            hh = p * in_pair + j
            gain = jnp.where(lane // head_width == j, skip_ref[hh], gain)
            mix = (scores[g] * decay[hh]).astype(BF16)
            result = result + dot(mix, x2 * head_masks[j])
        local[:, at] = result + gain * x2.astype(F32)
        return carry

    def pass_state(c):
        @pl.when(z > 0)
        def _():
            state_copy(c).wait_recv()

            @pl.when(z < n - 1)
            def _():
                end = ec[c, tokens - 1 :, :]
                s_out[c] = (end * s_in[c].astype(F32) + s_loc[c]).astype(BF16)
                state_copy(c).start()

    def pass_adjoint(c):
        @pl.when(z < n - 1)
        def _():
            adjoint_copy(c).wait_recv()

            @pl.when(z > 0)
            def _():
                end = ec[c, tokens - 1 :, :]
                a_out[c] = (end * a_in[c].astype(F32) + a_loc[c]).astype(BF16)
                adjoint_copy(c).start()

    def gradient_copy(zp, g, kind, up):
        to = z + 1 if up else z - 1
        at = (zp * groups + g) * 2 + kind
        cols = pl.ds(pl.multiple_of(kind * STATE, STATE), STATE)
        return pltpu.make_async_remote_copy(
            g_all.at[zp, g, :, cols], g_all.at[zp, g, :, cols],
            send_g.at[up * 2 * n * groups + at], recv_g.at[at],
            device_id=place(to, h), device_id_type=MESH,
        )

    def pass_gradient(zp, g, kind):
        @pl.when(jnp.logical_and(zp <= z, z < n - 1))
        def _():
            gradient_copy(zp, g, kind, 1).start()

        @pl.when(jnp.logical_and(zp >= z, z > 0))
        def _():
            gradient_copy(zp, g, kind, 0).start()

    def take_gradient(zp, g, second):
        upper = 2 * zp // n
        kind = second * upper + (1 - second) * (1 - upper)
        at = (zp * groups + g) * 2 + kind
        cols = pl.ds(pl.multiple_of(kind * STATE, STATE), STATE)
        pltpu.make_async_remote_copy(
            g_all.at[zp, g, :, cols], g_all.at[zp, g, :, cols],
            send_g.at[0], recv_g.at[at],
            device_id=across(1), device_id_type=MESH,
        ).wait_recv()
        pass_gradient(zp, g, kind)


    def take_near(g, second):
        take_gradient(nearest(1), g, second)

        @pl.when(between)
        def _():
            take_gradient(nearest(2), g, second)

    def take_far(g, second):
        def take(i, carry):
            @pl.when(jnp.logical_not(jnp.logical_and(between, i == 2)))
            def _():
                take_gradient(nearest(i), g, second)
            return carry

        lax.fori_loop(2, n, take, 0)

    def chain_end(c, second):
        @pl.when((2 * z < n) != second)
        def _():
            pass_state(c)

        @pl.when((2 * z < n) == second)
        def _():
            pass_adjoint(c)

    def carried_terms(g, ref, factors, carried):
        total = ref[g]
        for c in range(g * group_chunks, (g + 1) * group_chunks):
            total = total + dot(factors[c], carried[c], LANES_BOTH)
        return total.astype(BF16)

    def send_gradient(g, second):
        @pl.when((2 * z < n) != second)
        def _():
            g_all[z, g, :, STATE:] = carried_terms(g, g_read, ys, s_in)
            pass_gradient(z, g, 1)

        @pl.when((2 * z < n) == second)
        def _():
            g_all[z, g, :, :STATE] = carried_terms(g, g_write, xs, a_in)
            pass_gradient(z, g, 0)

    def begin(g):
        def collect(zs, carry):
            adjacent = at_least(zs + 1, z) * at_least(z + 1, zs)

            @pl.when(jnp.logical_and(zs != z, merges(zs, z) + adjacent > 0))
            def _():
                part_arrival(n + zs, g)
                acc[g] = acc[g] + part_in[g, n + zs].astype(F32)
            return carry

        lax.fori_loop(0, n, collect, 0)
        write[g] = acc[g, :, :STATE].astype(BF16)
        read[g] = acc[g, :, STATE:].astype(BF16)
        lax.fori_loop(g * group_chunks, (g + 1) * group_chunks, block_states, 0)
        scores[g] = dot(read[g], write[g], LANES_BOTH)
        mixed = mix_sum[g].astype(BF16)
        g_write[g] = dot(mixed, read[g], ROWS_FIRST)
        g_read[g] = dot(mixed, write[g])

    last = groups - 1
    begin(0)

    @pl.when(jnp.logical_not(between))
    def _():
        for g in range(1, groups):
            product(token_block(1), g)

    ahead = group_chunks // 2
    for g in range(groups + 1):

        def chain(i, carry):
            if g > 0:
                before = (g - 1) * group_chunks + i

                done = group_chunks if g == groups and groups > 1 else ahead

                @pl.when(jnp.logical_not(jnp.logical_and(between, i < done)))
                def _():
                    chain_end(before, True)

            if g < groups:
                c = g * group_chunks + i
                chain_end(c, False)
                if g == 0:

                    @pl.when(jnp.logical_and(between, i >= group_chunks - ahead))
                    def _():
                        chain_end(c - (group_chunks - ahead), True)

                lax.fori_loop(c * chunk_pairs, (c + 1) * chunk_pairs, mixing, 0)
            return carry

        lax.fori_loop(0, group_chunks, chain, 0)
        if g > 0:
            if g == groups and groups > 1:

                @pl.when(jnp.logical_not(between))
                def _():
                    send_gradient(last, True)

            else:
                send_gradient(g - 1, True)
        if g < groups:
            if g > 0:
                count = group_chunks if g == last else ahead

                @pl.when(between)
                def _():
                    def chain_ahead(c, carry):
                        chain_end(c, True)
                        return carry

                    start = g * group_chunks
                    lax.fori_loop(start, start + count, chain_ahead, 0)
                    if g == last:
                        send_gradient(g, True)

            send_gradient(g, False)
        if g + 1 < groups:
            begin(g + 1)
        if g > 0 and g < groups:
            take_near(g - 1, 0)

    def finish(c, carry):
        at = pl.ds(pl.multiple_of(c * chunk_width, chunk_width), chunk_width)
        carried = dot(read[c // group_chunks], s_in[c])
        out[:, at] = (local[:, at] + ec[c] * carried).astype(BF16)
        return carry

    def gradient_store(g):
        cols = pl.ds(g * 2 * STATE, 2 * STATE)
        return pltpu.make_async_copy(
            grad_low.at[:, cols], grad_hbm.at[:, cols], store_sem.at[2 + g]
        )

    def keep_gradient(g):
        grad_low[:, g * 2 * STATE : (g + 1) * 2 * STATE] = grad[g].astype(BF16)
        gradient_store(g).start()

    def own_terms(g):
        grad[g] = dot(held_t[z], g_all[z, g])

    def add_term(i, g):
        zp = nearest(i)
        grad[g] = grad[g] + dot(held_t[zp], g_all[zp, g])

    def add_terms(g):
        def add(i, carry):
            add_term(i, g)
            return carry

        lax.fori_loop(1, n, add, 0)

    def late_terms(i, carry):
        @pl.when(jnp.logical_not(jnp.logical_and(between, i == 2)))
        def _():
            take_gradient(nearest(i), last, 1)
            add_term(i, last)
        return carry

    for g in range(last):
        take_far(g, 0)
        take_near(g, 1)
    take_near(last, 0)
    lax.fori_loop(0, chunks, finish, 0)
    out_store = pltpu.make_async_copy(out, out_hbm, store_sem.at[0])
    out_store.start()
    for g in range(last):
        take_far(g, 1)
    take_far(last, 0)
    take_near(last, 1)
    for g in range(last):
        own_terms(g)
        add_terms(g)
        keep_gradient(g)
    own_terms(last)
    add_term(1, last)

    @pl.when(between)
    def _():
        add_term(2, last)

    lax.fori_loop(2, n, late_terms, 0)
    keep_gradient(last)

    def drain_features(i, carry):
        c, j = i // per_device, i % per_device
        for k in range(heads_axis):
            mine, _, remote = feature_parts(k, j, c)
            if k > 0:
                relay_copy(k, j, c).wait_send()

            @pl.when(jnp.logical_not(mine))
            def _():
                remote.wait_send()
        return carry

    lax.fori_loop(0, per_device * subs, drain_features, 0)

    def drain(d, carry):
        zp = (z + d) % n
        for k in range(1, heads_axis):
            share(zp, k).wait_send()
        for k in range(heads_axis):
            hand_over(zp, k, sub, 1 - sub).wait_send()

        for g in range(groups):

            @pl.when(zp != z)
            def _():
                part_copy(zp, g).wait_send()

            for kind in range(2):

                @pl.when(jnp.logical_and(zp <= z, z < n - 1))
                def _():
                    gradient_copy(zp, g, kind, 1).wait_send()

                @pl.when(jnp.logical_and(zp >= z, z > 0))
                def _():
                    gradient_copy(zp, g, kind, 0).wait_send()
        return carry

    lax.fori_loop(0, n, drain, 0)

    def drain_chain(c, carry):
        @pl.when(z < n - 1)
        def _():
            state_copy(c).wait_send()

        @pl.when(z > 0)
        def _():
            adjoint_copy(c).wait_send()
        return carry

    lax.fori_loop(0, chunks, drain_chain, 0)
    out_store.wait()

    code_store.wait()
    for g in range(groups):
        gradient_store(g).wait()


def update(
    scale, tile, master_in, code_in, grad_in, out_in, new_hbm, sparse_hbm, out_hbm,
    master, code, grad, out, new_ref, sparse_ref, load_sem, store_sem,
):
    rows, columns = master.shape
    steps = rows // tile
    slab = out.shape[0] // steps

    def part(i, size):
        return pl.ds(pl.multiple_of(i * size, size), size)

    def loads(i):
        pairs = ((master_in, master, tile), (code_in, code, tile), (grad_in, grad, tile), (out_in, out, slab))
        return [
            pltpu.make_async_copy(
                src.at[part(i, size), :], dst.at[part(i, size), :], load_sem.at[4 * i + j]
            )
            for j, (src, dst, size) in enumerate(pairs)
        ]

    def stores(i):
        pairs = ((new_ref, new_hbm, tile), (sparse_ref, sparse_hbm, tile), (out, out_hbm, slab))
        return [
            pltpu.make_async_copy(
                src.at[part(i, size), :], dst.at[part(i, size), :], store_sem.at[3 * i + j]
            )
            for j, (src, dst, size) in enumerate(pairs)
        ]

    def begin(i, carry):
        for load in loads(i):
            load.start()
        return carry

    lax.fori_loop(0, steps, begin, 0)
    place_in = lax.broadcasted_iota(jnp.int32, (tile, columns), 0) % 4

    def step(i, carry):
        for load in loads(i):
            load.wait()
        at = part(i, tile)
        bits = code[at, :].astype(F32).astype(jnp.int32) >> place_in
        keep = (bits & 1).astype(F32)
        keep_next = ((bits >> 4) & 1).astype(F32)
        old = master[at, :]
        new = old - LEARN_RATE * (
            grad[at, :].astype(F32) * scale + WEIGHT_DECAY * (1.0 - keep) * old
        )
        new_ref[at, :] = new
        sparse_ref[at, :] = (new * keep_next).astype(BF16)
        for store in stores(i):
            store.start()
        return carry

    lax.fori_loop(0, steps, step, 0)

    def finish(i, carry):
        for store in stores(i):
            store.wait()
        return carry

    lax.fori_loop(0, steps, finish, 0)


def on_device(
    n, heads_axis, subs,
    hidden, inner_values, log_decay, skip_gain, cotangent, master, mask_now, mask_next,
):
    hs = heads_axis * subs
    tokens, features = hidden.shape
    rows, columns = master.shape
    width = inner_values.shape[1]
    heads = log_decay.shape[1]
    groups = columns // (2 * STATE)
    chunks = 4 * groups
    chunk_width = width // chunks
    per_device = features // rows
    scale = 2.0 / math.sqrt(features * hs)
    vmem = pl.BlockSpec(memory_space=pltpu.VMEM)
    hbm = pl.BlockSpec(memory_space=pl.ANY)
    dma = pltpu.SemaphoreType.DMA
    V = pltpu.VMEM
    out, grad, code = pl.pallas_call(
        functools.partial(kernel, n, heads_axis, subs, scale),
        out_shape=(
            jax.ShapeDtypeStruct((tokens, width), BF16),
            jax.ShapeDtypeStruct((rows, columns), BF16),
            jax.ShapeDtypeStruct((rows, columns), BF16),
        ),
        in_specs=[hbm, hbm, hbm, vmem, pl.BlockSpec(memory_space=pltpu.SMEM), hbm, hbm, hbm],
        out_specs=(hbm, hbm, hbm),
        scratch_shapes=[
            V((tokens, width), BF16),
            V((rows, columns), BF16),
            V((tokens, width), BF16),
            V((tokens, width), BF16),
            V((rows, columns), F32),
            V((rows // 4, columns), jnp.int32),
            V((rows // 4, columns), jnp.int32),
            V((rows, columns), BF16),
            V((rows, columns), BF16),
            V((n, tokens, rows), BF16),
            V((n, rows, tokens), BF16),
            V((groups, n, tokens, 2 * STATE), BF16),
            V((groups, 2 * n, tokens, 2 * STATE), BF16),
            V((groups, tokens, 2 * STATE), F32),
            V((tokens, LANES), F32),
            V((LANES, tokens), F32),
            V((heads, tokens, tokens), F32),
            V((groups, tokens, tokens), F32),
            V((chunks, tokens, chunk_width), BF16),
            V((chunks, tokens, chunk_width), BF16),
            V((chunks, tokens, chunk_width), F32),
            V((groups, tokens, STATE), BF16),
            V((groups, tokens, STATE), BF16),
            V((groups, tokens, tokens), F32),
            V((chunks, STATE, chunk_width), F32),
            V((chunks, STATE, chunk_width), F32),
            V((chunks, STATE, chunk_width), BF16),
            V((chunks, STATE, chunk_width), BF16),
            V((chunks, STATE, chunk_width), BF16),
            V((chunks, STATE, chunk_width), BF16),
            V((groups, tokens, STATE), F32),
            V((groups, tokens, STATE), F32),
            V((n, groups, tokens, 2 * STATE), BF16),
            V((groups, rows, 2 * STATE), F32),
            V((tokens, width), F32),
            V(((heads_axis - 1) * per_device * subs, tokens // hs, rows), BF16),
            dma((5,)),
            dma((1,)),
            dma(((heads_axis - 1) * per_device * subs,)),
            dma(((heads_axis - 1) * per_device * subs,)),
            dma((per_device * hs,)),
            dma((n,)),
            dma((n * heads_axis,)),
            dma((n * heads_axis,)),
            dma((n * heads_axis,)),
            dma((n * heads_axis,)),
            dma((groups * n,)),
            dma((groups * 2 * n,)),
            dma((chunks,)),
            dma((chunks,)),
            dma((chunks,)),
            dma((chunks,)),
            dma((4 * n * groups,)),
            dma((2 * n * groups,)),
            dma((2 + groups,)),
        ],
        compiler_params=pltpu.CompilerParams(
            collective_id=0, has_side_effects=True, vmem_limit_bytes=58 * 1024 * 1024
        ),
        name="layer_step",
    )(hidden, inner_values, cotangent, log_decay.T, skip_gain, master, mask_now, mask_next)
    tile = max(rows // 4, 16)
    steps = rows // tile
    new, sparse, out = pl.pallas_call(
        functools.partial(update, scale, tile),
        out_shape=(
            jax.ShapeDtypeStruct((rows, columns), F32),
            jax.ShapeDtypeStruct((rows, columns), BF16),
            jax.ShapeDtypeStruct((tokens, width), BF16),
        ),
        in_specs=[hbm, hbm, hbm, hbm],
        out_specs=(hbm, hbm, hbm),
        scratch_shapes=[
            V((rows, columns), F32),
            V((rows, columns), BF16),
            V((rows, columns), BF16),
            V((tokens, width), BF16),
            V((rows, columns), F32),
            V((rows, columns), BF16),
            dma((4 * steps,)),
            dma((3 * steps,)),
        ],
        compiler_params=pltpu.CompilerParams(vmem_limit_bytes=58 * 1024 * 1024),
        name="weight_update",
    )(master, code, grad, out)
    return out, new, sparse


def solution(mesh):
    spread = P(("grp", "seq"), ("head", "sub"))
    weights = P("seq", ("head", "sub"))
    return jax.shard_map(
        functools.partial(
            on_device, mesh.shape["seq"], mesh.shape["head"], mesh.shape["sub"]
        ),
        mesh=mesh,
        in_specs=(
            spread, spread, spread, P(("head", "sub")), spread, weights, weights, weights
        ),
        out_specs=(spread, spread, spread),
        check_vma=False,
    )
```

```python
import functools
import math

import jax
import jax.numpy as jnp
from jax import lax
from jax.experimental import pallas as pl
from jax.experimental.pallas import tpu as pltpu
from jax.sharding import PartitionSpec as P

STATE = 128
LEARN_RATE = 0.05
WEIGHT_DECAY = 10.0
LANES = 128
MESH = pl.DeviceIdType.MESH
F32 = jnp.float32
BF16 = jnp.bfloat16

ROWS_FIRST = (((0,), (0,)), ((), ()))
LANES_BOTH = (((1,), (1,)), ((), ()))


def dot(a, b, dims=None):
    if dims is None:
        dims = (((1,), (0,)), ((), ()))
    return lax.dot_general(a, b, dims, preferred_element_type=F32)


def pattern_code(ids):
    code = jnp.where(ids == 0, 3.0, 12.0)
    code = jnp.where(ids == 1, 5.0, code)
    code = jnp.where(ids == 2, 9.0, code)
    code = jnp.where(ids == 3, 6.0, code)
    return jnp.where(ids == 4, 10.0, code)


def kernel(
    n, heads_axis, subs, scale,
    hid, x_in, dy_in, log_ref, skip_ref, master_in, now_in, next_in,
    out_hbm, grad_hbm, code_hbm,
    out, grad_low,
    xv, dyv, master, now, nxt, code, eff,
    held, held_t, part_out, part_in, acc,
    cum, cum_t, decay, mix_sum, xs, ys, ec, write, read, scores,
    s_loc, a_loc, s_out, a_out, s_in, a_in, g_write, g_read, g_all, grad, local,
    relay, load_sem, own_sem, send_r, recv_r, send1, recv1, send2, recv2, send3, recv3, send_p, recv_p,
    send_s, recv_s, send_a, recv_a, send_g, recv_g, store_sem,
):
    hs = heads_axis * subs
    tokens = hid.shape[0]
    part = tokens // hs
    rows, columns = master.shape
    per_device = hid.shape[1] // rows
    groups = columns // (2 * STATE)
    width = xv.shape[1]
    heads = log_ref.shape[0]
    head_width = width // heads
    in_pair = LANES // head_width
    pairs = width // LANES
    chunks, _, chunk_width = xs.shape
    chunk_pairs = chunk_width // LANES
    group_chunks = chunks // groups
    group_pairs = pairs // groups

    z = lax.axis_index("seq")
    sub = lax.axis_index("sub")
    h = lax.axis_index("head") * subs + sub
    me = z * hs + h
    upper_half = 2 * z // n
    inward = upper_half * (n - 1 - z) + (1 - upper_half) * z

    def at_least(a, b):
        return (a + 2 * n - b) // (2 * n)

    def farthest(i):
        both = 1 - at_least(i, 2 * inward)
        step = both * (i // 2) + (1 - both) * (i - inward)
        down = both * (i % 2)
        to = down * step + (1 - down) * (n - 1 - step)
        return upper_half * (n - 1 - to) + (1 - upper_half) * to

    def nearest(i):
        return farthest(n - 1 - i)

    def place(zz, hh):
        return {"seq": zz, "head": hh // subs, "sub": hh % subs}

    loads = [
        pltpu.make_async_copy(src, dst, load_sem.at[i])
        for i, (src, dst) in enumerate(
            ((x_in, xv), (dy_in, dyv), (now_in, now), (next_in, nxt), (master_in, master))
        )
    ]
    for load in loads[2:]:
        load.start()

    barrier = pltpu.get_barrier_semaphore()

    def same_line(i):
        return place(i // subs, h - sub + i % subs)

    def greet_line(i, carry):
        @pl.when(i != z * subs + sub)
        def _():
            pl.semaphore_signal(barrier, inc=1, device_id=same_line(i), device_id_type=MESH)
        return carry

    def across(k):
        return place(z, (h // subs + k) % heads_axis * subs + sub)

    for k in range(1, heads_axis):
        pl.semaphore_signal(barrier, inc=1, device_id=across(k), device_id_type=MESH)
    lax.fori_loop(0, n * subs, greet_line, 0)
    pl.semaphore_wait(barrier, n * subs - 1 + heads_axis - 1)

    def quarter(t):
        return pl.ds(pl.multiple_of(t * part, part), part)

    def plane(j):
        return pl.ds(pl.multiple_of(j * rows, rows), rows)

    def relay_copy(k, j, c):
        at = ((k - 1) * per_device + j) * subs + c
        t = (h // subs + k) % heads_axis * subs + c
        return pltpu.make_async_remote_copy(
            hid.at[quarter(t), plane(j)], relay.at[at], send_r.at[at], recv_r.at[at],
            device_id=across(k), device_id_type=MESH,
        )

    def feature_parts(k, j, c):
        t = h - sub + c
        source = ((h // subs + heads_axis - k) % heads_axis) * subs + sub
        zt = source * per_device + j
        if k == 0:
            src = hid.at[quarter(t), plane(j)]
        else:
            src = relay.at[((k - 1) * per_device + j) * subs + c]
        dst = held.at[z, quarter(t), :]
        mine = jnp.logical_and(zt == z, c == sub)
        local_copy = pltpu.make_async_copy(src, dst, own_sem.at[0])
        remote = pltpu.make_async_remote_copy(
            src, dst, send1.at[(k * per_device + j) * subs + c], recv1.at[z],
            device_id=place(zt, t), device_id_type=MESH,
        )
        return mine, local_copy, remote

    def send_features(k, j, c):
        mine, local_copy, remote = feature_parts(k, j, c)

        @pl.when(mine)
        def _():
            local_copy.start()

        @pl.when(jnp.logical_not(mine))
        def _():
            remote.start()

    def forward_features(c):
        def forward(j, carry):
            for k in range(1, heads_axis):
                relay_copy(k, j, c).wait_recv()
                send_features(k, j, c)
            return carry

        lax.fori_loop(0, per_device, forward, 0)

    def first_relays(i, carry):
        for k in range(1, heads_axis):
            relay_copy(k, i % per_device, i // per_device).start()
        return carry

    def first_sends(i, carry):
        send_features(0, i % per_device, i // per_device)
        return carry

    lax.fori_loop(0, per_device * subs, first_relays, 0)
    lax.fori_loop(0, per_device * subs, first_sends, 0)
    for load in loads[:2]:
        load.start()

    at_row = lax.broadcasted_iota(jnp.int32, (tokens, tokens), 0)
    at_lane = lax.broadcasted_iota(jnp.int32, (tokens, tokens), 1)
    upper = (at_row <= at_lane).astype(F32)
    cum_t[...] = jnp.zeros_like(cum_t)
    cum_t[:heads, :] = lax.dot_general(
        log_ref[...], upper, (((1,), (0,)), ((), ())),
        precision=lax.Precision.HIGHEST, preferred_element_type=F32,
    )
    cum[...] = cum_t[...].T

    loads[2].wait()
    loads[3].wait()
    loads[4].wait()
    small = (pattern_code(now[...]) + 16.0 * pattern_code(nxt[...])).astype(BF16)
    tile = min(rows, 128)

    def effective(i, carry):
        at = pl.ds(pl.multiple_of(i * tile, tile), tile)
        row = i * tile + lax.broadcasted_iota(jnp.int32, (tile, rows // 4), 0)
        spot = lax.broadcasted_iota(jnp.int32, (tile, rows // 4), 1)
        spread = (row // 4 == spot).astype(BF16)
        both = dot(spread, small)
        place_in = lax.broadcasted_iota(jnp.int32, (tile, columns), 0) % 4
        bits = both.astype(jnp.int32) >> place_in
        keep = (bits & 1).astype(F32)
        decayed = 1.0 - LEARN_RATE * WEIGHT_DECAY * (1.0 - keep)
        code[at, :] = jnp.where((bits & 16) > 0, decayed, -decayed).astype(BF16)
        eff[at, :] = (master[at, :] * keep * scale).astype(BF16)
        return carry

    lax.fori_loop(0, rows // tile, effective, 0)
    code_store = pltpu.make_async_copy(code, code_hbm, store_sem.at[1])
    code_store.start()

    loads[0].wait()
    loads[1].wait()
    mix_sum[...] = jnp.zeros_like(mix_sum)
    lane = lax.broadcasted_iota(jnp.int32, (tokens, LANES), 1)
    head_masks = [
        (lane // head_width == j).astype(BF16) for j in range(in_pair)
    ]

    def head_column(hh):
        return jnp.sum(jnp.where(lane == hh, cum[...], 0.0), axis=1, keepdims=True)

    def independent(p, carry):
        at = pl.ds(pl.multiple_of(p * LANES, LANES), LANES)
        c = p // chunk_pairs
        inner = pl.ds(pl.multiple_of((p % chunk_pairs) * LANES, LANES), LANES)
        x2, d2 = xv[:, at], dyv[:, at]
        total = jnp.zeros((tokens, tokens), F32)
        across = jnp.zeros((tokens, LANES), F32)
        for j in range(in_pair):
            hh = p * in_pair + j
            column = head_column(hh)
            across = jnp.where(lane // head_width == j, column, across)
            spread = column - cum_t[pl.ds(hh, 1), :]
            factor = jnp.exp(jnp.where(at_row >= at_lane, spread, -1e30))
            decay[hh] = factor
            total = total + dot(d2 * head_masks[j], x2, LANES_BOTH) * factor
        g = p // group_pairs
        mix_sum[g] = mix_sum[g] + total
        grown = jnp.exp(across)
        left = jnp.exp(across[tokens - 1 :, :] - across)
        ec[c, :, inner] = grown
        xs[c, :, inner] = (x2.astype(F32) * left).astype(BF16)
        ys[c, :, inner] = (d2.astype(F32) * grown).astype(BF16)
        return carry

    from_h = z // per_device
    between = jnp.logical_and(z > 0, z < n - 1)

    def share(zp, k):
        head = (h // subs + k) % heads_axis
        return pltpu.make_async_remote_copy(
            held.at[zp, quarter(h), :], held.at[zp, quarter(h), :],
            send2.at[zp * heads_axis + k], recv2.at[zp * heads_axis + k],
            device_id=place(z, head * subs + sub), device_id_type=MESH,
        )

    def shared(zp, k):
        t = ((h // subs + heads_axis - k) % heads_axis) * subs + sub
        return pltpu.make_async_remote_copy(
            held.at[zp, quarter(t), :], held.at[zp, quarter(t), :],
            send2.at[zp * heads_axis + k], recv2.at[zp * heads_axis + k],
            device_id=place(z, t), device_id_type=MESH,
        )

    def hand_over(zp, k, from_sub, to_sub):
        t = ((h // subs + heads_axis - k) % heads_axis) * subs + from_sub
        return pltpu.make_async_remote_copy(
            held.at[zp, quarter(t), :], held.at[zp, quarter(t), :],
            send3.at[zp * heads_axis + k], recv3.at[zp * heads_axis + k],
            device_id=place(z, h - sub + to_sub), device_id_type=MESH,
        )

    outer = at_least(inward, 1)
    skipped = outer * (2 * inward - 1) + (1 - outer) * (n - 2)

    def token_block(d):
        i = d - 2
        far = farthest(i + at_least(i, skipped))
        own = 1 - at_least(d, 1)
        first = at_least(d, 1) * (1 - at_least(d, 2))
        return own * z + first * farthest(skipped) + at_least(d, 2) * far

    def arrived(d):
        zp = token_block(d)
        mine = jnp.logical_and(zp == z, from_h % subs == sub)

        @pl.when(mine)
        def _():
            pltpu.make_async_copy(
                held.at[zp, quarter(h), :], held.at[zp, quarter(h), :], own_sem.at[0]
            ).wait()

        @pl.when(jnp.logical_not(mine))
        def _():
            pltpu.make_async_remote_copy(
                held.at[zp, quarter(h), :], held.at[zp, quarter(h), :],
                send1.at[0], recv1.at[zp],
                device_id=place(z, h - sub + 1 - sub), device_id_type=MESH,
            ).wait_recv()

        for k in range(1, heads_axis):
            share(zp, k).start()
        hand_over(zp, 0, sub, 1 - sub).start()

    def crossed(d):
        zp = token_block(d)
        for k in range(1, heads_axis):
            shared(zp, k).wait_recv()
            hand_over(zp, k, sub, 1 - sub).start()

    for c in range(subs):
        forward_features(c)
    arrived(0)
    lax.fori_loop(0, pairs // 2, independent, 0)
    arrived(1)
    crossed(0)
    lax.fori_loop(pairs // 2, pairs, independent, 0)
    arrived(2)


    def merges(zs, t):
        up = at_least(t, zs)
        return up * (zs % 2) + (1 - up) * ((n - 1 - zs) % 2)

    def part_copy(t, g):
        merged = merges(z, t)
        to = merged * t + (1 - merged) * (z + 2 * at_least(t, z) - 1)
        final = at_least(t, to) * at_least(to, t)
        slot = final * (n + z) + (1 - final) * t
        return pltpu.make_async_remote_copy(
            part_out.at[g, t], part_in.at[g, slot],
            send_p.at[g * n + t], recv_p.at[g * 2 * n + slot],
            device_id=place(to, h), device_id_type=MESH,
        )

    def part_arrival(slot, g):
        pltpu.make_async_remote_copy(
            part_in.at[g, slot], part_in.at[g, slot],
            send_p.at[0], recv_p.at[g * 2 * n + slot],
            device_id=across(1), device_id_type=MESH,
        ).wait_recv()

    def own_product(g):
        acc[g] = dot(held[z], eff[:, g * 2 * STATE : (g + 1) * 2 * STATE])

    def product(t, g):
        result = dot(held[t], eff[:, g * 2 * STATE : (g + 1) * 2 * STATE])
        merged = merges(z, t)

        @pl.when(merged == 0)
        def _():
            part_out[g, t] = result.astype(BF16)

        @pl.when(merged == 1)
        def _():
            part_arrival(t, g)
            part_out[g, t] = (result + part_in[g, t].astype(F32)).astype(BF16)

        part_copy(t, g).start()

    def ready(d):
        zp = token_block(d)
        for k in range(heads_axis):
            hand_over(zp, k, 1 - sub, sub).wait_recv()
        return zp

    crossed(1)
    ready(0)
    for g in range(groups):
        own_product(g)

    def project(d, carry):
        @pl.when(d + 1 < n)
        def _():
            arrived(d + 1)

        product(ready(d - 1), 0)
        crossed(d)
        return carry

    lax.fori_loop(2, n, project, 0)
    product(ready(n - 1), 0)
    for g in range(1, groups):

        def later_product(d, carry):
            product(token_block(d), g)
            return carry

        lax.fori_loop(2, n, later_product, 0)

        @pl.when(between)
        def _():
            product(token_block(1), g)


    def turn(zp, carry):
        held_t[zp] = held[zp].T
        return carry

    lax.fori_loop(0, n, turn, 0)

    def state_copy(c):
        return pltpu.make_async_remote_copy(
            s_out.at[c], s_in.at[c], send_s.at[c], recv_s.at[c],
            device_id=place(lax.rem(z + 1, n), h), device_id_type=MESH,
        )

    def adjoint_copy(c):
        return pltpu.make_async_remote_copy(
            a_out.at[c], a_in.at[c], send_a.at[c], recv_a.at[c],
            device_id=place(lax.rem(z + n - 1, n), h), device_id_type=MESH,
        )

    def block_states(c, carry):
        g = c // group_chunks
        state = dot(write[g], xs[c], ROWS_FIRST)
        adjoint = dot(read[g], ys[c], ROWS_FIRST)
        s_loc[c] = state
        a_loc[c] = adjoint

        @pl.when(z == 0)
        def _():
            s_in[c] = jnp.zeros_like(s_in[c])
            s_out[c] = state.astype(BF16)
            state_copy(c).start()

        @pl.when(z == n - 1)
        def _():
            a_in[c] = jnp.zeros_like(a_in[c])
            a_out[c] = adjoint.astype(BF16)
            adjoint_copy(c).start()
        return carry

    def mixing(p, carry):
        at = pl.ds(pl.multiple_of(p * LANES, LANES), LANES)
        x2 = xv[:, at]
        g = p // group_pairs
        gain = jnp.zeros((tokens, LANES), F32)
        result = jnp.zeros((tokens, LANES), F32)
        for j in range(in_pair):
            hh = p * in_pair + j
            gain = jnp.where(lane // head_width == j, skip_ref[hh], gain)
            mix = (scores[g] * decay[hh]).astype(BF16)
            result = result + dot(mix, x2 * head_masks[j])
        local[:, at] = result + gain * x2.astype(F32)
        return carry

    def pass_state(c):
        @pl.when(z > 0)
        def _():
            state_copy(c).wait_recv()

            @pl.when(z < n - 1)
            def _():
                end = ec[c, tokens - 1 :, :]
                s_out[c] = (end * s_in[c].astype(F32) + s_loc[c]).astype(BF16)
                state_copy(c).start()

    def pass_adjoint(c):
        @pl.when(z < n - 1)
        def _():
            adjoint_copy(c).wait_recv()

            @pl.when(z > 0)
            def _():
                end = ec[c, tokens - 1 :, :]
                a_out[c] = (end * a_in[c].astype(F32) + a_loc[c]).astype(BF16)
                adjoint_copy(c).start()

    def gradient_copy(zp, g, kind, up):
        to = z + 1 if up else z - 1
        at = (zp * groups + g) * 2 + kind
        cols = pl.ds(pl.multiple_of(kind * STATE, STATE), STATE)
        return pltpu.make_async_remote_copy(
            g_all.at[zp, g, :, cols], g_all.at[zp, g, :, cols],
            send_g.at[up * 2 * n * groups + at], recv_g.at[at],
            device_id=place(to, h), device_id_type=MESH,
        )

    def pass_gradient(zp, g, kind):
        @pl.when(jnp.logical_and(zp <= z, z < n - 1))
        def _():
            gradient_copy(zp, g, kind, 1).start()

        @pl.when(jnp.logical_and(zp >= z, z > 0))
        def _():
            gradient_copy(zp, g, kind, 0).start()

    def take_gradient(zp, g, second):
        upper = 2 * zp // n
        kind = second * upper + (1 - second) * (1 - upper)
        at = (zp * groups + g) * 2 + kind
        cols = pl.ds(pl.multiple_of(kind * STATE, STATE), STATE)
        pltpu.make_async_remote_copy(
            g_all.at[zp, g, :, cols], g_all.at[zp, g, :, cols],
            send_g.at[0], recv_g.at[at],
            device_id=across(1), device_id_type=MESH,
        ).wait_recv()
        pass_gradient(zp, g, kind)


    def take_near(g, second):
        take_gradient(nearest(1), g, second)

        @pl.when(between)
        def _():
            take_gradient(nearest(2), g, second)

    def take_far(g, second):
        def take(i, carry):
            @pl.when(jnp.logical_not(jnp.logical_and(between, i == 2)))
            def _():
                take_gradient(nearest(i), g, second)
            return carry

        lax.fori_loop(2, n, take, 0)

    def chain_end(c, second):
        @pl.when((2 * z < n) != second)
        def _():
            pass_state(c)

        @pl.when((2 * z < n) == second)
        def _():
            pass_adjoint(c)

    def carried_terms(g, ref, factors, carried):
        total = ref[g]
        for c in range(g * group_chunks, (g + 1) * group_chunks):
            total = total + dot(factors[c], carried[c], LANES_BOTH)
        return total.astype(BF16)

    def send_gradient(g, second):
        @pl.when((2 * z < n) != second)
        def _():
            g_all[z, g, :, STATE:] = carried_terms(g, g_read, ys, s_in)
            pass_gradient(z, g, 1)

        @pl.when((2 * z < n) == second)
        def _():
            g_all[z, g, :, :STATE] = carried_terms(g, g_write, xs, a_in)
            pass_gradient(z, g, 0)

    def begin(g):
        def collect(zs, carry):
            adjacent = at_least(zs + 1, z) * at_least(z + 1, zs)

            @pl.when(jnp.logical_and(zs != z, merges(zs, z) + adjacent > 0))
            def _():
                part_arrival(n + zs, g)
                acc[g] = acc[g] + part_in[g, n + zs].astype(F32)
            return carry

        lax.fori_loop(0, n, collect, 0)
        write[g] = acc[g, :, :STATE].astype(BF16)
        read[g] = acc[g, :, STATE:].astype(BF16)
        lax.fori_loop(g * group_chunks, (g + 1) * group_chunks, block_states, 0)
        scores[g] = dot(read[g], write[g], LANES_BOTH)
        mixed = mix_sum[g].astype(BF16)
        g_write[g] = dot(mixed, read[g], ROWS_FIRST)
        g_read[g] = dot(mixed, write[g])

    last = groups - 1
    begin(0)

    @pl.when(jnp.logical_not(between))
    def _():
        for g in range(1, groups):
            product(token_block(1), g)

    ahead = group_chunks // 2
    for g in range(groups + 1):

        def chain(i, carry):
            if g > 0:
                before = (g - 1) * group_chunks + i

                done = group_chunks if g == groups and groups > 1 else ahead

                @pl.when(jnp.logical_not(jnp.logical_and(between, i < done)))
                def _():
                    chain_end(before, True)

            if g < groups:
                c = g * group_chunks + i
                chain_end(c, False)
                if g == 0:

                    @pl.when(jnp.logical_and(between, i >= group_chunks - ahead))
                    def _():
                        chain_end(c - (group_chunks - ahead), True)

                lax.fori_loop(c * chunk_pairs, (c + 1) * chunk_pairs, mixing, 0)
            return carry

        lax.fori_loop(0, group_chunks, chain, 0)
        if g > 0:
            if g == groups and groups > 1:

                @pl.when(jnp.logical_not(between))
                def _():
                    send_gradient(last, True)

            else:
                send_gradient(g - 1, True)
        if g < groups:
            if g > 0:
                count = group_chunks if g == last else ahead

                @pl.when(between)
                def _():
                    def chain_ahead(c, carry):
                        chain_end(c, True)
                        return carry

                    start = g * group_chunks
                    lax.fori_loop(start, start + count, chain_ahead, 0)
                    if g == last:
                        send_gradient(g, True)

            send_gradient(g, False)
        if g + 1 < groups:
            begin(g + 1)
        if g > 0 and g < groups:
            take_near(g - 1, 0)

    def finish(c, carry):
        at = pl.ds(pl.multiple_of(c * chunk_width, chunk_width), chunk_width)
        carried = dot(read[c // group_chunks], s_in[c])
        out[:, at] = (local[:, at] + ec[c] * carried).astype(BF16)
        return carry

    def gradient_store(g):
        cols = pl.ds(g * 2 * STATE, 2 * STATE)
        return pltpu.make_async_copy(
            grad_low.at[:, cols], grad_hbm.at[:, cols], store_sem.at[2 + g]
        )

    def keep_gradient(g):
        grad_low[:, g * 2 * STATE : (g + 1) * 2 * STATE] = grad[g].astype(BF16)
        gradient_store(g).start()

    def own_terms(g):
        grad[g] = dot(held_t[z], g_all[z, g])

    def add_term(i, g):
        zp = nearest(i)
        grad[g] = grad[g] + dot(held_t[zp], g_all[zp, g])

    def add_terms(g):
        def add(i, carry):
            add_term(i, g)
            return carry

        lax.fori_loop(1, n, add, 0)

    def late_terms(i, carry):
        @pl.when(jnp.logical_not(jnp.logical_and(between, i == 2)))
        def _():
            take_gradient(nearest(i), last, 1)
            add_term(i, last)
        return carry

    for g in range(last):
        take_far(g, 0)
        take_near(g, 1)
    take_near(last, 0)
    lax.fori_loop(0, chunks, finish, 0)
    out_store = pltpu.make_async_copy(out, out_hbm, store_sem.at[0])
    out_store.start()
    for g in range(last):
        take_far(g, 1)
    take_far(last, 0)
    take_near(last, 1)
    for g in range(last):
        own_terms(g)
        add_terms(g)
        keep_gradient(g)
    own_terms(last)
    add_term(1, last)

    @pl.when(between)
    def _():
        add_term(2, last)

    lax.fori_loop(2, n, late_terms, 0)
    keep_gradient(last)

    def drain_features(i, carry):
        c, j = i // per_device, i % per_device
        for k in range(heads_axis):
            mine, _, remote = feature_parts(k, j, c)
            if k > 0:
                relay_copy(k, j, c).wait_send()

            @pl.when(jnp.logical_not(mine))
            def _():
                remote.wait_send()
        return carry

    lax.fori_loop(0, per_device * subs, drain_features, 0)

    def drain(d, carry):
        zp = (z + d) % n
        for k in range(1, heads_axis):
            share(zp, k).wait_send()
        for k in range(heads_axis):
            hand_over(zp, k, sub, 1 - sub).wait_send()

        for g in range(groups):

            @pl.when(zp != z)
            def _():
                part_copy(zp, g).wait_send()

            for kind in range(2):

                @pl.when(jnp.logical_and(zp <= z, z < n - 1))
                def _():
                    gradient_copy(zp, g, kind, 1).wait_send()

                @pl.when(jnp.logical_and(zp >= z, z > 0))
                def _():
                    gradient_copy(zp, g, kind, 0).wait_send()
        return carry

    lax.fori_loop(0, n, drain, 0)

    def drain_chain(c, carry):
        @pl.when(z < n - 1)
        def _():
            state_copy(c).wait_send()

        @pl.when(z > 0)
        def _():
            adjoint_copy(c).wait_send()
        return carry

    lax.fori_loop(0, chunks, drain_chain, 0)
    out_store.wait()

    code_store.wait()
    for g in range(groups):
        gradient_store(g).wait()


def update(
    scale, tile, master_in, code_in, grad_in, out_in, new_hbm, sparse_hbm, out_hbm,
    master, code, grad, out, new_ref, sparse_ref, load_sem, store_sem,
):
    rows, columns = master.shape
    steps = rows // tile

    def part(i, size):
        return pl.ds(pl.multiple_of(i * size, size), size)

    def loads(i):
        pairs = ((master_in, master, tile), (code_in, code, tile), (grad_in, grad, tile))
        return [
            pltpu.make_async_copy(
                src.at[part(i, size), :], dst.at[part(i, size), :], load_sem.at[3 * i + j]
            )
            for j, (src, dst, size) in enumerate(pairs)
        ]

    def stores(i):
        pairs = ((new_ref, new_hbm, tile), (sparse_ref, sparse_hbm, tile))
        return [
            pltpu.make_async_copy(
                src.at[part(i, size), :], dst.at[part(i, size), :], store_sem.at[2 * i + j]
            )
            for j, (src, dst, size) in enumerate(pairs)
        ]

    def begin(i, carry):
        for load in loads(i):
            load.start()
        return carry

    lax.fori_loop(0, steps, begin, 0)

    def out_load(i):
        at = part(i, out.shape[0] // 2)
        return pltpu.make_async_copy(
            out_in.at[at, :], out.at[at, :], load_sem.at[3 * steps + i]
        )

    def out_store(i):
        at = part(i, out.shape[0] // 2)
        return pltpu.make_async_copy(
            out.at[at, :], out_hbm.at[at, :], store_sem.at[2 * steps + i]
        )

    for i in range(2):
        out_load(i).start()
    def step(i, carry):
        for load in loads(i):
            load.wait()
        at = part(i, tile)
        factor = code[at, :].astype(F32)
        gradient = grad[at, :].astype(F32)
        new = master[at, :] * jnp.abs(factor) - (LEARN_RATE * scale) * gradient
        new_ref[at, :] = new
        sparse_ref[at, :] = jnp.where(factor > 0, new, 0.0).astype(BF16)
        for store in stores(i):
            store.start()
        return carry

    lax.fori_loop(0, steps, step, 0)
    for i in range(2):
        out_load(i).wait()
        out_store(i).start()

    def finish(i, carry):
        for store in stores(i):
            store.wait()
        return carry

    lax.fori_loop(0, steps, finish, 0)
    for i in range(2):
        out_store(i).wait()


def on_device(
    n, heads_axis, subs,
    hidden, inner_values, log_decay, skip_gain, cotangent, master, mask_now, mask_next,
):
    hs = heads_axis * subs
    tokens, features = hidden.shape
    rows, columns = master.shape
    width = inner_values.shape[1]
    heads = log_decay.shape[1]
    groups = columns // (2 * STATE)
    chunks = 4 * groups
    chunk_width = width // chunks
    per_device = features // rows
    scale = 2.0 / math.sqrt(features * hs)
    vmem = pl.BlockSpec(memory_space=pltpu.VMEM)
    hbm = pl.BlockSpec(memory_space=pl.ANY)
    dma = pltpu.SemaphoreType.DMA
    V = pltpu.VMEM
    out, grad, code = pl.pallas_call(
        functools.partial(kernel, n, heads_axis, subs, scale),
        out_shape=(
            jax.ShapeDtypeStruct((tokens, width), BF16),
            jax.ShapeDtypeStruct((rows, columns), BF16),
            jax.ShapeDtypeStruct((rows, columns), BF16),
        ),
        in_specs=[hbm, hbm, hbm, vmem, pl.BlockSpec(memory_space=pltpu.SMEM), hbm, hbm, hbm],
        out_specs=(hbm, hbm, hbm),
        scratch_shapes=[
            V((tokens, width), BF16),
            V((rows, columns), BF16),
            V((tokens, width), BF16),
            V((tokens, width), BF16),
            V((rows, columns), F32),
            V((rows // 4, columns), jnp.int32),
            V((rows // 4, columns), jnp.int32),
            V((rows, columns), BF16),
            V((rows, columns), BF16),
            V((n, tokens, rows), BF16),
            V((n, rows, tokens), BF16),
            V((groups, n, tokens, 2 * STATE), BF16),
            V((groups, 2 * n, tokens, 2 * STATE), BF16),
            V((groups, tokens, 2 * STATE), F32),
            V((tokens, LANES), F32),
            V((LANES, tokens), F32),
            V((heads, tokens, tokens), F32),
            V((groups, tokens, tokens), F32),
            V((chunks, tokens, chunk_width), BF16),
            V((chunks, tokens, chunk_width), BF16),
            V((chunks, tokens, chunk_width), F32),
            V((groups, tokens, STATE), BF16),
            V((groups, tokens, STATE), BF16),
            V((groups, tokens, tokens), F32),
            V((chunks, STATE, chunk_width), F32),
            V((chunks, STATE, chunk_width), F32),
            V((chunks, STATE, chunk_width), BF16),
            V((chunks, STATE, chunk_width), BF16),
            V((chunks, STATE, chunk_width), BF16),
            V((chunks, STATE, chunk_width), BF16),
            V((groups, tokens, STATE), F32),
            V((groups, tokens, STATE), F32),
            V((n, groups, tokens, 2 * STATE), BF16),
            V((groups, rows, 2 * STATE), F32),
            V((tokens, width), F32),
            V(((heads_axis - 1) * per_device * subs, tokens // hs, rows), BF16),
            dma((5,)),
            dma((1,)),
            dma(((heads_axis - 1) * per_device * subs,)),
            dma(((heads_axis - 1) * per_device * subs,)),
            dma((per_device * hs,)),
            dma((n,)),
            dma((n * heads_axis,)),
            dma((n * heads_axis,)),
            dma((n * heads_axis,)),
            dma((n * heads_axis,)),
            dma((groups * n,)),
            dma((groups * 2 * n,)),
            dma((chunks,)),
            dma((chunks,)),
            dma((chunks,)),
            dma((chunks,)),
            dma((4 * n * groups,)),
            dma((2 * n * groups,)),
            dma((2 + groups,)),
        ],
        compiler_params=pltpu.CompilerParams(
            collective_id=0, has_side_effects=True, vmem_limit_bytes=58 * 1024 * 1024
        ),
        name="layer_step",
    )(hidden, inner_values, cotangent, log_decay.T, skip_gain, master, mask_now, mask_next)
    tile = max(rows // 4, 16)
    steps = rows // tile
    new, sparse, out = pl.pallas_call(
        functools.partial(update, scale, tile),
        out_shape=(
            jax.ShapeDtypeStruct((rows, columns), F32),
            jax.ShapeDtypeStruct((rows, columns), BF16),
            jax.ShapeDtypeStruct((tokens, width), BF16),
        ),
        in_specs=[hbm, hbm, hbm, hbm],
        out_specs=(hbm, hbm, hbm),
        scratch_shapes=[
            V((rows, columns), F32),
            V((rows, columns), BF16),
            V((rows, columns), BF16),
            V((tokens, width), BF16),
            V((rows, columns), F32),
            V((rows, columns), BF16),
            dma((3 * steps + 2,)),
            dma((2 * steps + 2,)),
        ],
        compiler_params=pltpu.CompilerParams(vmem_limit_bytes=58 * 1024 * 1024),
        name="weight_update",
    )(master, code, grad, out)
    return out, new, sparse


def solution(mesh):
    spread = P(("grp", "seq"), ("head", "sub"))
    weights = P("seq", ("head", "sub"))
    return jax.shard_map(
        functools.partial(
            on_device, mesh.shape["seq"], mesh.shape["head"], mesh.shape["sub"]
        ),
        mesh=mesh,
        in_specs=(
            spread, spread, spread, P(("head", "sub")), spread, weights, weights, weights
        ),
        out_specs=(spread, spread, spread),
        check_vma=False,
    )
```
